32 devices in a mesh: row: 4 (over y, x), col: 8 (over z, core).
Axes of the slice: x: 2, y: 2, z: 4, core: 2. Of those that a mesh axis runs over, the one named last changes fastest.
Arguments:
- rhs: float32 [32, 32768], P(None, ('row', 'col')), may hold values from -22 to 22
- precond: float32 [32, 1024, 1024], P(('row', 'col')), may hold values from -0.2 to 2.6, as said below
- design_t: bfloat16 [32768, 3072], P('row', 'col'), may hold values from -0.046875 to 0.046875
- terrain: float32 [32768], P(('row', 'col')), may hold values from 0.25 to 2.5
- order_slot: int32 [32768], P(('row', 'col')), may hold values from 0 to 1023, as said below
- degree_source: int32 [32768], P('row'), may hold values from 0 to 8191, as said below
Outputs:
- solution: float32 [32, 32768], P(None, ('row', 'col'))
- residual: float32 [32, 32768], P(None, ('row', 'col'))
The draws below stay inside these ranges and needn't reach their ends.
Inputs may be any that keep to these rules, and one draw needn't show every extreme that they name: Within each block of 1024 order-wise parameters, order_slot is a permutation of 0 to 1023. Within each parameter block of 8192 degree-wise parameters, degree_source is a permutation of 0 to 8191. `precond`: each block is symmetric positive definite.
All inputs are finite; a program needn't handle non-finite values.
Results may differ from the reference program's by a relative error of at most 0.007.
Values may be sent and summed in bfloat16 or wider, within the bound.
A program may use at most 128 MiB of HBM per device.

```python
import math
import jax
import jax.numpy as jnp
from jax import lax

BLK = 1024
K = 32
ITERS = 3
NBLK = 32
NORD = 32768
OBS = 3072
PARAMB = 8192
PIECE = 256
N_ROW = 4


def draw_rhs(key, part):
    key_base, key_scale = jax.random.split(key, 2)
    spots = jnp.arange(NORD, dtype=jnp.float32) / NORD
    trend = jnp.exp(spots * math.log(3.0))
    rough = jnp.exp(jax.random.uniform(key_scale, (NORD,), jnp.float32, 0.0, math.log(10.0)))
    scale = 0.1 * trend * rough
    values = jnp.clip(jax.random.normal(key_base, (K, NORD), jnp.float32), -6.0, 6.0) * scale[None, :]
    return values.astype(jnp.float32)


def draw_precond(key, part):
    key_diag, key_off = jax.random.split(key, 2)
    diagonal = jnp.exp(jax.random.uniform(key_diag, (NBLK, BLK), jnp.float32, 0.0, math.log(1.3)))
    if BLK >= 256:
        spread = 0.6 / math.sqrt(BLK)
    else:
        spread = 0.95 / (BLK - 1)
    upper = jax.random.uniform(key_off, (NBLK, BLK, BLK), jnp.float32, -spread, spread)
    rows = jnp.arange(BLK)[:, None]
    cols = jnp.arange(BLK)[None, :]
    above = (rows < cols).astype(jnp.float32)
    ident = (rows == cols).astype(jnp.float32)
    symmetric = upper * above[None] + jnp.swapaxes(upper * above[None], 1, 2)
    matrix = symmetric + ident[None] * diagonal[:, :, None]
    return matrix.astype(jnp.float32)


def draw_order_slot(key, part):
    bits = jax.random.randint(jax.random.fold_in(key, 5), (NBLK, BLK), 0, 2 ** 30 // BLK)
    scores = bits * BLK + jnp.arange(BLK, dtype=jnp.int32)[None, :]
    slots = jnp.argsort(scores, axis=1)
    return slots.reshape(NORD).astype(jnp.int32)


def draw_degree_source(key, part):
    bits = jax.random.randint(jax.random.fold_in(key, 9), (NORD // PARAMB, PARAMB), 0, 2 ** 30 // PARAMB)
    scores = bits * PARAMB + jnp.arange(PARAMB, dtype=jnp.int32)[None, :]
    sources = jnp.argsort(scores, axis=1)
    return sources.reshape(NORD).astype(jnp.int32)


def raised(array, key, source, target, parts, factor):
    owner, partner = [(jnp.arange(array.shape[position]) // (array.shape[position] // parts)).reshape([-1 if axis == position else 1 for axis in range(array.ndim)]) for position in (source, target)]
    chosen = jax.random.permutation(key, parts)[partner]
    strong = (owner == chosen) | (owner == (partner + parts // 2) % parts)
    return jnp.where(strong, factor * array, array)


def level_of(own_key, dims, pieces, smallest, top_value):
    def one(dim, parts):
        steps = jax.random.uniform(jax.random.fold_in(jax.random.fold_in(own_key, 6), dim), (parts,), jnp.float32, smallest / len(pieces), top_value / len(pieces))
        return jnp.repeat(jnp.exp(steps), dims[dim] // parts).reshape((-1,) + (1,) * (len(dims) - dim - 1))

    level = one(*pieces[0])
    for cut in pieces[1:]:
        level = level * one(*cut)
    return level


def bell_draw_with(stream_key, extent, deviation, bound, shards, heavy, held_as=jnp.bfloat16):
    values = deviation * jax.random.normal(stream_key, extent, jnp.float32)
    if shards:
        values = values * level_of(stream_key, extent, shards, -0.22, 0.18)
    return jnp.clip(raised(values, jax.random.fold_in(stream_key, 3), *heavy), -bound, bound).astype(held_as)


def setup_inputs(seed: int = 0) -> dict:
    splits = jax.random.split(jax.random.key(seed), 7)
    rhs = draw_rhs(jax.random.fold_in(splits[6], 71), 0)
    precond = draw_precond(jax.random.fold_in(splits[6], 71), 0)
    design_t = bell_draw_with(splits[2], (NORD, OBS), NORD ** -0.5, 0.046875, ((0, 4), (1, 8)), (1, 0, 8, 2.0))
    terrain = jnp.clip(jnp.exp(math.log(2.5) - 2.3025851 * jax.random.uniform(splits[3], (NORD,), jnp.float32) ** level_of(splits[3], (NORD,), ((0, 32),), -0.2, 0.2)), 0.25, 2.5)
    order_slot = draw_order_slot(jax.random.fold_in(splits[6], 71), 0)
    degree_source = draw_degree_source(jax.random.fold_in(splits[6], 71), 0)
    return {"rhs": rhs, "precond": precond, "design_t": design_t, "terrain": terrain, "order_slot": order_slot, "degree_source": degree_source}


def spd_solve(matrix, right):
    sym = 0.5 * (matrix + matrix.T)
    lower = jnp.linalg.cholesky(sym)
    half = lax.linalg.triangular_solve(lower, right, left_side=True, lower=True)
    return lax.linalg.triangular_solve(lower, half, left_side=True, lower=True, transpose_a=True)

def inner_gram(left, right):
    return lax.dot_general(left, right, (((1,), (1,)), ((), ())), precision=lax.Precision.HIGHEST)

def combine_rows(coeff, vectors):
    return jnp.dot(coeff.T, vectors, precision=lax.Precision.HIGHEST)

def remap_index(order_slot, degree_source):
    entries = jnp.arange(NORD, dtype=jnp.int32)
    block_of = entries // BLK
    inv_slot = jnp.zeros((NORD,), jnp.int32).at[block_of * BLK + order_slot].set(entries % BLK)
    param_block = entries // PARAMB
    owner = degree_source // PIECE
    within = degree_source % PIECE
    ord_index = owner * BLK + inv_slot[owner * BLK + param_block * PIECE + within]
    deg_index = jnp.zeros((NORD,), jnp.int32).at[ord_index].set(entries)
    return (ord_index, deg_index)

def reference(rhs, precond, design_t, terrain, order_slot, degree_source):
    ord_index, deg_index = remap_index(order_slot, degree_source)
    blocks = design_t.reshape(N_ROW, PARAMB, OBS)

    def operate(vector):
        lowered = vector.astype(jnp.bfloat16)
        spread = lowered[:, ord_index].reshape(K, N_ROW, PARAMB).transpose(1, 0, 2)

        def add_block(total, pair):
            return (total + jnp.dot(pair[0].astype(jnp.float32), pair[1].astype(jnp.float32), preferred_element_type=jnp.float32), None)
        observed, _ = lax.scan(add_block, jnp.zeros((K, OBS), jnp.float32), (spread, blocks))
        observed = observed.astype(jnp.bfloat16)
        terms = lax.map(lambda block: lax.dot_general(observed.astype(jnp.float32), block.astype(jnp.float32), (((1,), (1,)), ((), ())), preferred_element_type=jnp.float32), blocks)
        terms = terms.transpose(1, 0, 2).reshape(K, NORD)
        return terms[:, deg_index] + terrain[None, :] * vector

    def precondition(vector):
        shaped = vector.reshape(K, NBLK, BLK)
        return jnp.einsum('kbi,bij->kbj', shaped, precond, precision=lax.Precision.HIGHEST).reshape(K, NORD)
    solution = jnp.zeros_like(rhs)
    residual = rhs
    precon = precondition(residual)
    direction = precon
    gamma = inner_gram(precon, residual)
    for step in range(ITERS):
        image = operate(direction)
        alpha = spd_solve(inner_gram(direction, image), gamma)
        solution = solution + combine_rows(alpha, direction)
        residual = residual - combine_rows(alpha, image)
        if step + 1 < ITERS:
            precon = precondition(residual)
            gamma_next = inner_gram(precon, residual)
            beta = spd_solve(gamma, gamma_next)
            direction = precon + combine_rows(beta, direction)
            gamma = gamma_next
    return (solution, residual)
```

```python
import functools

import jax
import jax.numpy as jnp
from jax import lax
from jax.experimental import pallas as pl
from jax.experimental.pallas import tpu as pltpu
from jax.sharding import PartitionSpec as P

ITERS = 3
F32 = jnp.float32
BF16 = jnp.bfloat16
HIGH = lax.Precision.HIGHEST
NT = (((1,), (1,)), ((), ()))
NN = (((1,), (0,)), ((), ()))


def dot(a, b, dims=NN, precision=None):
    return lax.dot_general(a, b, dims, precision=precision, preferred_element_type=F32)


def split(x):
    hi = x.astype(BF16)
    return hi, (x - hi.astype(F32)).astype(BF16)


def pack(gram):
    count = gram.shape[0]
    rows = count * count // 128
    return jnp.concatenate([gram[i * rows : (i + 1) * rows] for i in range(count // rows)], axis=1)


def unpack(packed, count):
    return jnp.concatenate(
        [packed[:, i * count : (i + 1) * count] for i in range(packed.shape[1] // count)], axis=0
    )


def inverses(mats):
    count = mats[0].shape[0]
    eye = (
        lax.broadcasted_iota(jnp.int32, (count, count), 0)
        == lax.broadcasted_iota(jnp.int32, (count, count), 1)
    )
    eye = jnp.where(eye, 1.0, 0.0).astype(F32)
    rows = lax.broadcasted_iota(jnp.int32, (count, 2 * count), 0)
    work = [jnp.concatenate([m, eye], axis=1) for m in mats]
    for k in range(count):
        nxt = []
        for m in work:
            row = m[k : k + 1, :] / m[k : k + 1, k : k + 1]
            nxt.append(jnp.where(rows == k, row, m - m[:, k : k + 1] * row))
        work = nxt
    return [m[:, count:] for m in work]


def kernel(
    nr, nc, fused, rhs, precond, design_hbm, terrain, slot, source, out, design, design_sem,
    stage, ring, phi, plo, qt, direction, seen,
    arr, wbuf, obuf, psend, precv, zsend, zrecv,
    tbuf, cbuf, grow, gcol, send_sem, recv_sem,
):
    count, width = rhs.shape
    piece = width // nr
    ng = nc // 2
    r = lax.axis_index("row")
    c = lax.axis_index("col")
    g = c // 2
    core = c % 2
    used = [0]
    sent = []

    def send(src, dst, row, col):
        i = used[0]
        used[0] += 1
        copy = pltpu.make_async_remote_copy(
            src_ref=src, dst_ref=dst, send_sem=send_sem.at[i], recv_sem=recv_sem.at[i],
            device_id=(row, col), device_id_type=pl.DeviceIdType.MESH,
        )
        copy.start()
        sent.append(copy)
        return copy

    fetch = pltpu.make_async_copy(design_hbm, design, design_sem)
    fetch.start()
    sol, res = out.at[0], out.at[1]
    barrier = pltpu.get_barrier_semaphore()
    peers = [
        ((r + i) % nr, ((g + d) % ng) * 2 + core) for i in range(nr) for d in range(ng) if i or d
    ] + [(r, ((g + d) % ng) * 2 + 1 - core) for d in range(ng)]
    for peer in peers:
        pl.semaphore_signal(barrier, inc=1, device_id=peer, device_id_type=pl.DeviceIdType.MESH)

    step_rows = 128

    @pl.loop(0, width // step_rows)
    def _(i):
        at = pl.ds(pl.multiple_of(i * step_rows, step_rows), step_rows)
        hi, lo = split(precond[0, at, :])
        phi[at, :] = hi
        plo[at, :] = lo
        ids = lax.broadcasted_iota(jnp.int32, (step_rows, width), 0) + i * step_rows
        qt[at, :] = jnp.where(ids == slot[...], 1.0, 0.0).astype(BF16)

    def precondition(v):
        hi, lo = split(v)
        both = dot(jnp.concatenate([hi, lo], axis=0), phi[...])
        return both[:count] + both[count:] + dot(hi, plo[...])

    def gram(a, b):
        prod = dot(jnp.concatenate(a, axis=0), jnp.concatenate(b, axis=0), NT)
        rows = prod[:count]
        for i in range(1, len(a)):
            rows = rows + prod[i * count : (i + 1) * count]
        total = rows[:, :count]
        for i in range(1, len(b)):
            total = total + rows[:, i * count : (i + 1) * count]
        return total

    def sym_gram(a, b):
        return 0.5 * (gram(a, b) + gram(b, a))

    def rows_out(buf, packed):
        buf[r] = packed
        return [send(buf.at[r], buf.at[r], (r + d) % nr, c) for d in range(1, nr)]

    def cols_out(buf, packed):
        buf[c] = packed
        return [send(buf.at[c], buf.at[c], r, (c + d) % nc) for d in range(1, nc)]

    def collect(copies, buf, n):
        for copy in copies:
            copy.wait_recv()
        total = buf[0]
        for i in range(1, n):
            total = total + buf[i]
        return total

    def block(col):
        return design[pl.ds(pl.multiple_of(col * width, width), width), :]

    def place():
        rows, obs = design.shape
        lanes = obs // 128
        chunk = 512
        flat = stage.reshape(4 * rows, 128)

        @pl.loop(0, rows // chunk)
        def _(i):
            at = pl.multiple_of(i * chunk, chunk)
            for j in range(lanes):
                part = design[pl.ds(at, chunk), j * 128 : (j + 1) * 128].astype(F32)
                flat[pl.ds(at * 4 + j, chunk, stride=4), :] = part

        group = ring.shape[0] // 4

        @pl.loop(0, rows // group)
        def _(i):
            at = pl.multiple_of(i * group, group)
            for k in range(group):
                ring[4 * k : 4 * k + 4, :] = stage[source[at + k]]
            for j in range(lanes):
                part = ring[pl.ds(j, group, stride=4), :]
                design[pl.ds(at, group), j * 128 : (j + 1) * 128] = part.astype(BF16)

    residual = rhs[...]
    precon = precondition(residual)
    sol[...] = jnp.zeros_like(rhs)
    res[...] = residual
    pl.semaphore_wait(barrier, len(peers))
    gamma = gamma_inv = None

    for it in range(ITERS):
        arranged = dot(precon.astype(BF16), qt[...], NT).astype(BF16)
        for i in range(nr):
            arr[it, i] = arranged[:, i * piece : (i + 1) * piece]
        mine = wbuf.at[it, 0, 0]
        mine[r] = arr[it, r]
        order = list(range(1, ng)) + [0]
        moves = {d: [] for d in order}
        for d in order:
            for i in range(nr):
                if i or d:
                    to = (r + i) % nr
                    there = ((g + d) % ng) * 2 + core
                    moves[d].append(send(arr.at[it, to], wbuf.at[it, d, 0, r], to, there))
        gamma_rows = rows_out(grow.at[it], pack(sym_gram(split(precon), split(residual))))

        def terrain_out():
            scaled = terrain[...] * direction[...]
            return rows_out(tbuf.at[it], pack(gram(split(direction[...]), split(scaled))))

        if it == 0:
            direction[...] = precon
            terrain_rows = terrain_out()
            fetch.wait()
            if fused:
                place()
        for copy in moves[0]:
            copy.wait_recv()
        near = [send(mine, wbuf.at[it, 0, 1], r, g * 2 + 1 - core)]

        def product(d, k):
            lhs = jnp.concatenate([wbuf[it, d, k, i] for i in range(nr)], axis=1)
            return dot(lhs, block(((g + ng - d) % ng) * 2 + (core + k) % 2))

        partial = product(0, 0)
        for d in range(1, ng):
            for copy in moves[d]:
                copy.wait_recv()
            near.append(send(wbuf.at[it, d, 0], wbuf.at[it, d, 1], r, g * 2 + 1 - core))
            partial = partial + product(d, 0)
            if d == ng // 2:
                gamma_cols = cols_out(gcol.at[it], collect(gamma_rows, grow.at[it], nr))
        for d in range(ng):
            near[d].wait_recv()
            partial = partial + product(d, 1)

        observed_rows = rows_out(obuf.at[it], partial)
        if it:
            gamma = unpack(collect(gamma_cols, gcol.at[it], nc), count)
            beta_t = dot(gamma, gamma_inv, NN, HIGH)
            direction[...] = precon + dot(beta_t, direction[...], NN, HIGH)
            terrain_rows = terrain_out()
            carried = dot(beta_t, seen[...], NN, HIGH)
        observed = collect(observed_rows, obuf.at[it], nr)
        if it:
            observed = observed + carried
        if it + 1 < ITERS:
            seen[...] = observed
        rounded = observed.astype(BF16)
        pairs = [None] * ng

        def pair_out(d):
            psend[it, d] = dot(rounded, block(((g + d) % ng) * 2 + 1 - core), NT)
            pairs[d] = send(psend.at[it, d], precv.at[it, d], r, g * 2 + 1 - core)

        for d in order[:2]:
            pair_out(d)
        curve = sym_gram(split(observed), (rounded,))
        curve = curve + unpack(collect(terrain_rows, tbuf.at[it], nr), count)
        curve_cols = cols_out(cbuf.at[it], pack(curve))
        zs = []
        for n, d in enumerate(order):
            own = dot(rounded, block(((g + d) % ng) * 2 + core), NT)
            if n + 2 < ng:
                pair_out(order[n + 2])
            pairs[d].wait_recv()
            own = own + precv[it, d]
            for i in range(nr):
                zsend[it, d, i] = own[:, i * piece : (i + 1) * piece].astype(BF16)
            for i in range(nr):
                if i or d:
                    to = (r + i) % nr
                    there = ((g + d) % ng) * 2 + core
                    zs.append(send(zsend.at[it, d, to], zrecv.at[it, d, r], to, there))
        zrecv[it, 0, r] = zsend[it, 0, r]
        if it == 0:
            gamma = unpack(collect(gamma_cols, gcol.at[0], nc), count)
        curve = unpack(collect(curve_cols, cbuf.at[it], nc), count)
        if it + 1 < ITERS:
            curve_inv, gamma_inv = inverses([curve, gamma])
        else:
            (curve_inv,) = inverses([curve])
        alpha_t = dot(gamma, curve_inv, NN, HIGH)
        sol[...] += dot(alpha_t, direction[...], NN, HIGH)
        for copy in zs:
            copy.wait_recv()
        pieces = []
        for i in range(nr):
            total = zrecv[it, 0, i].astype(F32)
            for d in range(1, ng):
                total = total + zrecv[it, d, i].astype(F32)
            pieces.append(total)
        arrived = jnp.concatenate(pieces, axis=1)
        both = dot(jnp.concatenate(split(arrived), axis=0), qt[...])
        image = both[:count] + both[count:] + terrain[...] * direction[...]
        residual = res[...] - dot(alpha_t, image, NN, HIGH)
        res[...] = residual
        if it + 1 < ITERS:
            precon = precondition(residual)

    for copy in sent:
        copy.wait_send()


def part_kernel(both, sol, res):
    sol[...] = both[0]
    res[...] = both[1]


def bits(n):
    assert n & (n - 1) == 0
    return n.bit_length() - 1


def source_kernel(nr, nc, piece, wanted, out):
    rows = wanted.shape[1]
    high = rows // 128
    chunk = 1024

    def step(i, total):
        at = pl.multiple_of(i * chunk, chunk)
        w = wanted[:, pl.ds(at, chunk)]
        owner = w >> bits(piece)
        pos = ((owner & (nc - 1)) * nr + (owner >> bits(nc))) * piece + (w & (piece - 1))
        here = lax.broadcasted_iota(jnp.int32, (high, chunk), 1) + i * chunk
        hit = lax.broadcasted_iota(jnp.int32, (high, chunk), 0) == (pos >> 7)
        upper = jnp.where(hit, (here >> 7).astype(F32), 0.0)
        lower = jnp.where(hit, (here & 127).astype(F32), 0.0)
        lhs = jnp.concatenate([upper, lower], axis=0).astype(BF16)
        lane = lax.broadcasted_iota(jnp.int32, (128, chunk), 0) == (pos & 127)
        return total + dot(lhs, jnp.where(lane, 1.0, 0.0).astype(BF16), NT)

    total = lax.fori_loop(0, rows // chunk, step, jnp.zeros((2 * high, 128), F32))
    out[...] = (128.0 * total[:high] + total[high:]).astype(jnp.int32)


def source_rows(degree_source, nr, nc, piece):
    rows = degree_source.shape[0]
    vmem = pl.BlockSpec(memory_space=pltpu.VMEM)
    return pl.pallas_call(
        functools.partial(source_kernel, nr, nc, piece),
        out_shape=jax.ShapeDtypeStruct((rows // 128, 128), jnp.int32),
        in_specs=[vmem],
        out_specs=vmem,
    )(degree_source.reshape(1, rows)).reshape(rows)


def place_kernel(steps, chunk, lanes, pos, design, out, stage, placed):
    i = pl.program_id(0)

    @pl.when(i < steps)
    def _():
        for j in range(lanes):
            stage[pl.ds(j, chunk, stride=4), :] = design[:, j * 128 : (j + 1) * 128].astype(F32)
        base = i * chunk

        @pl.loop(0, chunk // 64)
        def _(n):
            for k in range(64):
                row = n * 64 + k
                to = pl.multiple_of(pos[base + row], 4)
                placed[pl.ds(to, 4), :] = stage[pl.ds(pl.multiple_of(row * 4, 4), 4), :]

    @pl.when(i >= steps)
    def _():
        base = pl.multiple_of((i - steps) * (chunk * 4), chunk * 4)
        for j in range(lanes):
            out[:, j * 128 : (j + 1) * 128] = placed[pl.ds(base + j, chunk, stride=4), :].astype(BF16)


def place_rows(design_t, pos):
    rows, obs = design_t.shape
    chunk = 512
    steps = rows // chunk
    return pl.pallas_call(
        functools.partial(place_kernel, steps, chunk, obs // 128),
        grid=(2 * steps,),
        out_shape=jax.ShapeDtypeStruct(design_t.shape, design_t.dtype),
        in_specs=[
            pl.BlockSpec(memory_space=pltpu.SMEM),
            pl.BlockSpec((chunk, obs), lambda i: (jnp.minimum(i, steps - 1), 0)),
        ],
        out_specs=pl.BlockSpec((chunk, obs), lambda i: (jnp.maximum(i - steps, 0), 0)),
        scratch_shapes=[pltpu.VMEM((4 * chunk, 128), F32), pltpu.VMEM((4 * rows, 128), F32)],
        compiler_params=pltpu.CompilerParams(vmem_limit_bytes=48 * 1024 * 1024),
    )(4 * pos, design_t)


def on_device(rhs, precond, design_t, terrain, order_slot, degree_source):
    nr = lax.axis_size("row")
    nc = lax.axis_size("col")
    count, width = rhs.shape
    piece = width // nr
    ng = nc // 2
    obs = design_t.shape[1]
    rows = design_t.shape[0]
    fused = rows <= 8192
    if fused:
        design_g = design_t
        source = source_rows(degree_source, nr, nc, piece)
    else:
        owner = degree_source // piece
        within = degree_source % piece
        design_g = place_rows(design_t, (owner % nc * nr + owner // nc) * piece + within)
        source = degree_source[:128]
    gram = (count * count // 128, 128)
    copies = ITERS * (2 * nr * ng + 3 * nr + 2 * nc + 2 * ng) + nr + nc
    vmem = pl.BlockSpec(memory_space=pltpu.VMEM)
    both = pl.pallas_call(
        functools.partial(kernel, nr, nc, fused),
        out_shape=jax.ShapeDtypeStruct((2,) + rhs.shape, F32),
        in_specs=[
            vmem, vmem, pl.BlockSpec(memory_space=pl.ANY), vmem, vmem,
            pl.BlockSpec(memory_space=pltpu.SMEM),
        ],
        out_specs=vmem,
        scratch_shapes=[
            pltpu.VMEM(design_t.shape, BF16),
            pltpu.SemaphoreType.DMA(()),
            pltpu.VMEM((rows if fused else 8, 4, 128), F32),
            pltpu.VMEM((512, 128), F32),
            pltpu.VMEM((width, width), BF16),
            pltpu.VMEM((width, width), BF16),
            pltpu.VMEM((width, width), BF16),
            pltpu.VMEM((count, width), F32),
            pltpu.VMEM((count, obs), F32),
            pltpu.VMEM((ITERS, nr, count, piece), BF16),
            pltpu.VMEM((ITERS, ng, 2, nr, count, piece), BF16),
            pltpu.VMEM((ITERS, nr, count, obs), F32),
            pltpu.VMEM((ITERS, ng, count, width), F32),
            pltpu.VMEM((ITERS, ng, count, width), F32),
            pltpu.VMEM((ITERS, ng, nr, count, piece), BF16),
            pltpu.VMEM((ITERS, ng, nr, count, piece), BF16),
            pltpu.VMEM((ITERS, nr) + gram, F32),
            pltpu.VMEM((ITERS, nc) + gram, F32),
            pltpu.VMEM((ITERS, nr) + gram, F32),
            pltpu.VMEM((ITERS, nc) + gram, F32),
            pltpu.SemaphoreType.DMA((copies,)),
            pltpu.SemaphoreType.DMA((copies,)),
        ],
        compiler_params=pltpu.CompilerParams(
            collective_id=0, has_side_effects=True, vmem_limit_bytes=60 * 1024 * 1024
        ),
    )(rhs, precond, design_g, terrain.reshape(1, width), order_slot.reshape(1, width), source)
    return pl.pallas_call(
        part_kernel,
        out_shape=(jax.ShapeDtypeStruct(rhs.shape, F32), jax.ShapeDtypeStruct(rhs.shape, F32)),
        in_specs=[vmem],
        out_specs=(vmem, vmem),
    )(both)


def solution(mesh):
    return jax.shard_map(
        on_device,
        mesh=mesh,
        in_specs=(
            P(None, ("row", "col")),
            P(("row", "col"), None, None),
            P("row", "col"),
            P(("row", "col")),
            P(("row", "col")),
            P("row"),
        ),
        out_specs=(P(None, ("row", "col")), P(None, ("row", "col"))),
        check_vma=False,
    )
```

```python
import functools

import jax
import jax.numpy as jnp
from jax import lax
from jax.experimental import pallas as pl
from jax.experimental.pallas import tpu as pltpu
from jax.sharding import PartitionSpec as P

ITERS = 3
PLACED = 6
F32 = jnp.float32
BF16 = jnp.bfloat16
HIGH = lax.Precision.HIGHEST
NT = (((1,), (1,)), ((), ()))
NN = (((1,), (0,)), ((), ()))


def dot(a, b, dims=NN, precision=None):
    return lax.dot_general(a, b, dims, precision=precision, preferred_element_type=F32)


def split(x):
    hi = x.astype(BF16)
    return hi, (x - hi.astype(F32)).astype(BF16)


def pack(gram):
    count = gram.shape[0]
    rows = count * count // 128
    return jnp.concatenate([gram[i * rows : (i + 1) * rows] for i in range(count // rows)], axis=1)


def unpack(packed, count):
    return jnp.concatenate(
        [packed[:, i * count : (i + 1) * count] for i in range(packed.shape[1] // count)], axis=0
    )


def inverses(mats):
    count = mats[0].shape[0]
    eye = (
        lax.broadcasted_iota(jnp.int32, (count, count), 0)
        == lax.broadcasted_iota(jnp.int32, (count, count), 1)
    )
    eye = jnp.where(eye, 1.0, 0.0).astype(F32)
    rows = lax.broadcasted_iota(jnp.int32, (count, 2 * count), 0)
    work = [jnp.concatenate([m, eye], axis=1) for m in mats]
    for k in range(count):
        nxt = []
        for m in work:
            row = m[k : k + 1, :] / m[k : k + 1, k : k + 1]
            nxt.append(jnp.where(rows == k, row, m - m[:, k : k + 1] * row))
        work = nxt
    return [m[:, count:] for m in work]


def kernel(
    nr, nc, fused, rhs, precond, design_hbm, terrain, slot, source, out, design, design_sem,
    stage, ring, phi, plo, qt, direction, seen,
    arr, wbuf, obuf, psend, precv, zsend, zrecv,
    tbuf, cbuf, grow, gcol, send_sem, recv_sem,
):
    count, width = rhs.shape
    piece = width // nr
    ng = nc // 2
    r = lax.axis_index("row")
    c = lax.axis_index("col")
    g = c // 2
    core = c % 2
    used = [0]
    sent = []

    def send(src, dst, row, col):
        i = used[0]
        used[0] += 1
        copy = pltpu.make_async_remote_copy(
            src_ref=src, dst_ref=dst, send_sem=send_sem.at[i], recv_sem=recv_sem.at[i],
            device_id=(row, col), device_id_type=pl.DeviceIdType.MESH,
        )
        copy.start()
        sent.append(copy)
        return copy

    fetch = pltpu.make_async_copy(design_hbm, design, design_sem)
    fetch.start()
    sol, res = out.at[0], out.at[1]
    barrier = pltpu.get_barrier_semaphore()
    peers = [
        ((r + i) % nr, ((g + d) % ng) * 2 + core) for i in range(nr) for d in range(ng) if i or d
    ] + [(r, ((g + d) % ng) * 2 + 1 - core) for d in range(ng)]
    for peer in peers:
        pl.semaphore_signal(barrier, inc=1, device_id=peer, device_id_type=pl.DeviceIdType.MESH)

    step_rows = 128

    @pl.loop(0, width // step_rows)
    def _(i):
        at = pl.ds(pl.multiple_of(i * step_rows, step_rows), step_rows)
        hi, lo = split(precond[0, at, :])
        phi[at, :] = hi
        plo[at, :] = lo
        ids = lax.broadcasted_iota(jnp.int32, (step_rows, width), 0) + i * step_rows
        qt[at, :] = jnp.where(ids == slot[...], 1.0, 0.0).astype(BF16)

    def precondition(v):
        hi, lo = split(v)
        both = dot(jnp.concatenate([hi, lo], axis=0), phi[...])
        return both[:count] + both[count:] + dot(hi, plo[...])

    def gram(a, b):
        prod = dot(jnp.concatenate(a, axis=0), jnp.concatenate(b, axis=0), NT)
        rows = prod[:count]
        for i in range(1, len(a)):
            rows = rows + prod[i * count : (i + 1) * count]
        total = rows[:, :count]
        for i in range(1, len(b)):
            total = total + rows[:, i * count : (i + 1) * count]
        return total

    def sym_gram(a, b):
        return 0.5 * (gram(a, b) + gram(b, a))

    def rows_out(buf, packed):
        buf[r] = packed.astype(buf.dtype)
        return [send(buf.at[r], buf.at[r], (r + d) % nr, c) for d in range(1, nr)]

    def cols_out(buf, packed):
        buf[c] = packed
        return [send(buf.at[c], buf.at[c], r, (c + d) % nc) for d in range(1, nc)]

    def collect(copies, buf, n):
        for copy in copies:
            copy.wait_recv()
        total = buf[0].astype(F32)
        for i in range(1, n):
            total = total + buf[i].astype(F32)
        return total

    def block(col):
        return design[pl.ds(pl.multiple_of(col * width, width), width), :]

    rows, obs = design.shape
    lanes = obs // 128
    group = ring.shape[0] // 4

    def fill():
        chunk = 512
        flat = stage.reshape(4 * rows, 128)

        @pl.loop(0, rows // chunk)
        def _(i):
            at = pl.multiple_of(i * chunk, chunk)
            for j in range(lanes):
                part = design[pl.ds(at, chunk), j * 128 : (j + 1) * 128].astype(F32)
                flat[pl.ds(at * 4 + j, chunk, stride=4), :] = part

    def place(begin, end):
        @pl.loop(begin, end)
        def _(i):
            at = pl.multiple_of(i * group, group)
            for k in range(group):
                ring[4 * k : 4 * k + 4, :] = stage[source[at + k]]
            for j in range(lanes):
                part = ring[pl.ds(j, group, stride=4), :]
                design[pl.ds(at, group), j * 128 : (j + 1) * 128] = part.astype(BF16)

    residual = rhs[...]
    precon = precondition(residual)
    sol[...] = jnp.zeros_like(rhs)
    res[...] = residual
    pl.semaphore_wait(barrier, len(peers))
    gamma = gamma_inv = None

    for it in range(ITERS):
        arranged = dot(precon.astype(BF16), qt[...], NT).astype(BF16)
        for i in range(nr):
            arr[it, i] = arranged[:, i * piece : (i + 1) * piece]
        mine = wbuf.at[it, 0, 0]
        mine[r] = arr[it, r]
        order = list(range(1, ng)) + [0]
        moves = {d: [] for d in order}
        for d in order:
            for i in range(nr):
                if i or d:
                    to = (r + i) % nr
                    there = ((g + d) % ng) * 2 + core
                    moves[d].append(send(arr.at[it, to], wbuf.at[it, d, 0, r], to, there))
        gamma_rows = rows_out(grow.at[it], pack(sym_gram(split(precon), split(residual))))

        def terrain_out():
            scaled = terrain[...] * direction[...]
            return rows_out(tbuf.at[it], pack(gram(split(direction[...]), split(scaled))))

        if it == 0:
            direction[...] = precon
            terrain_rows = terrain_out()
            fetch.wait()
            if fused:
                fill()
                place(0, rows // group * PLACED // 8)
        near = []

        def near_out(d):
            for copy in moves[d]:
                copy.wait_recv()
            near.append(send(wbuf.at[it, d, 0], wbuf.at[it, d, 1], r, g * 2 + 1 - core))

        if it == 0 and fused:
            for d in range(ng):
                near_out(d)
            place(rows // group * PLACED // 8, rows // group)
        else:
            near_out(0)

        def product(d, k):
            lhs = jnp.concatenate([wbuf[it, d, k, i] for i in range(nr)], axis=1)
            return dot(lhs, block(((g + ng - d) % ng) * 2 + (core + k) % 2))

        partial = product(0, 0)
        for d in range(1, ng):
            if len(near) == d:
                near_out(d)
            partial = partial + product(d, 0)
            if d == ng // 2:
                gamma_cols = cols_out(gcol.at[it], collect(gamma_rows, grow.at[it], nr))
        for d in range(ng):
            near[d].wait_recv()
            partial = partial + product(d, 1)

        observed_rows = rows_out(obuf.at[it], partial)
        if it:
            gamma = unpack(collect(gamma_cols, gcol.at[it], nc), count)
            beta_t = dot(gamma, gamma_inv, NN, HIGH)
            direction[...] = precon + dot(beta_t, direction[...], NN, HIGH)
            terrain_rows = terrain_out()
            carried = dot(beta_t, seen[...], NN, HIGH)
        observed = collect(observed_rows, obuf.at[it], nr)
        if it:
            observed = observed + carried
        if it + 1 < ITERS:
            seen[...] = observed
        rounded = observed.astype(BF16)
        pairs = [None] * ng

        def pair_out(d):
            psend[it, d] = dot(rounded, block(((g + d) % ng) * 2 + 1 - core), NT)
            pairs[d] = send(psend.at[it, d], precv.at[it, d], r, g * 2 + 1 - core)

        for d in order[:2]:
            pair_out(d)
        curve = sym_gram(split(observed), (rounded,))
        curve = curve + unpack(collect(terrain_rows, tbuf.at[it], nr), count)
        curve_cols = cols_out(cbuf.at[it], pack(curve))
        zs = []
        for n, d in enumerate(order):
            own = dot(rounded, block(((g + d) % ng) * 2 + core), NT)
            if n + 2 < ng:
                pair_out(order[n + 2])
            pairs[d].wait_recv()
            own = own + precv[it, d]
            for i in range(nr):
                zsend[it, d, i] = own[:, i * piece : (i + 1) * piece].astype(BF16)
            for i in range(nr):
                if i or d:
                    to = (r + i) % nr
                    there = ((g + d) % ng) * 2 + core
                    zs.append(send(zsend.at[it, d, to], zrecv.at[it, d, r], to, there))
        zrecv[it, 0, r] = zsend[it, 0, r]
        if it == 0:
            gamma = unpack(collect(gamma_cols, gcol.at[0], nc), count)
        curve = unpack(collect(curve_cols, cbuf.at[it], nc), count)
        if it + 1 < ITERS:
            curve_inv, gamma_inv = inverses([curve, gamma])
        else:
            (curve_inv,) = inverses([curve])
        alpha_t = dot(gamma, curve_inv, NN, HIGH)
        sol[...] += dot(alpha_t, direction[...], NN, HIGH)
        for copy in zs:
            copy.wait_recv()
        pieces = []
        for i in range(nr):
            total = zrecv[it, 0, i].astype(F32)
            for d in range(1, ng):
                total = total + zrecv[it, d, i].astype(F32)
            pieces.append(total)
        arrived = jnp.concatenate(pieces, axis=1)
        both = dot(jnp.concatenate(split(arrived), axis=0), qt[...])
        image = both[:count] + both[count:] + terrain[...] * direction[...]
        residual = res[...] - dot(alpha_t, image, NN, HIGH)
        res[...] = residual
        if it + 1 < ITERS:
            precon = precondition(residual)

    for copy in sent:
        copy.wait_send()


def part_kernel(both, sol, res):
    sol[...] = both[0]
    res[...] = both[1]


def bits(n):
    assert n & (n - 1) == 0
    return n.bit_length() - 1


def source_kernel(nr, nc, piece, wanted, out):
    rows = wanted.shape[1]
    high = rows // 128
    chunk = 1024

    def step(i, total):
        w = wanted[:, i * chunk : (i + 1) * chunk]
        owner = w >> bits(piece)
        pos = ((owner & (nc - 1)) * nr + (owner >> bits(nc))) * piece + (w & (piece - 1))
        here = lax.broadcasted_iota(jnp.int32, (high, chunk), 1) + i * chunk
        hit = lax.broadcasted_iota(jnp.int32, (high, chunk), 0) == (pos >> 7)
        upper = jnp.where(hit, (here >> 7).astype(F32), 0.0)
        lower = jnp.where(hit, (here & 127).astype(F32), 0.0)
        lhs = jnp.concatenate([upper, lower], axis=0).astype(BF16)
        lane = lax.broadcasted_iota(jnp.int32, (128, chunk), 0) == (pos & 127)
        return total + dot(lhs, jnp.where(lane, 1.0, 0.0).astype(BF16), NT)

    total = jnp.zeros((2 * high, 128), F32)
    for i in range(rows // chunk):
        total = step(i, total)
    out[...] = (128.0 * total[:high] + total[high:]).astype(jnp.int32)


def source_rows(degree_source, nr, nc, piece):
    rows = degree_source.shape[0]
    vmem = pl.BlockSpec(memory_space=pltpu.VMEM)
    return pl.pallas_call(
        functools.partial(source_kernel, nr, nc, piece),
        out_shape=jax.ShapeDtypeStruct((rows // 128, 128), jnp.int32),
        in_specs=[vmem],
        out_specs=vmem,
    )(degree_source.reshape(1, rows)).reshape(rows)


def place_kernel(steps, chunk, lanes, pos, design, out, stage, placed):
    i = pl.program_id(0)

    @pl.when(i < steps)
    def _():
        for j in range(lanes):
            stage[pl.ds(j, chunk, stride=4), :] = design[:, j * 128 : (j + 1) * 128].astype(F32)
        base = i * chunk

        @pl.loop(0, chunk // 64)
        def _(n):
            for k in range(64):
                row = n * 64 + k
                to = pl.multiple_of(pos[base + row], 4)
                placed[pl.ds(to, 4), :] = stage[pl.ds(pl.multiple_of(row * 4, 4), 4), :]

    @pl.when(i >= steps)
    def _():
        base = pl.multiple_of((i - steps) * (chunk * 4), chunk * 4)
        for j in range(lanes):
            out[:, j * 128 : (j + 1) * 128] = placed[pl.ds(base + j, chunk, stride=4), :].astype(BF16)


def place_rows(design_t, pos):
    rows, obs = design_t.shape
    chunk = 512
    steps = rows // chunk
    return pl.pallas_call(
        functools.partial(place_kernel, steps, chunk, obs // 128),
        grid=(2 * steps,),
        out_shape=jax.ShapeDtypeStruct(design_t.shape, design_t.dtype),
        in_specs=[
            pl.BlockSpec(memory_space=pltpu.SMEM),
            pl.BlockSpec((chunk, obs), lambda i: (jnp.minimum(i, steps - 1), 0)),
        ],
        out_specs=pl.BlockSpec((chunk, obs), lambda i: (jnp.maximum(i - steps, 0), 0)),
        scratch_shapes=[pltpu.VMEM((4 * chunk, 128), F32), pltpu.VMEM((4 * rows, 128), F32)],
        compiler_params=pltpu.CompilerParams(vmem_limit_bytes=48 * 1024 * 1024),
    )(4 * pos, design_t)


def on_device(rhs, precond, design_t, terrain, order_slot, degree_source):
    nr = lax.axis_size("row")
    nc = lax.axis_size("col")
    count, width = rhs.shape
    piece = width // nr
    ng = nc // 2
    obs = design_t.shape[1]
    rows = design_t.shape[0]
    fused = rows <= 8192
    if fused:
        design_g = design_t
        source = source_rows(degree_source, nr, nc, piece)
    else:
        owner = degree_source // piece
        within = degree_source % piece
        design_g = place_rows(design_t, (owner % nc * nr + owner // nc) * piece + within)
        source = degree_source[:128]
    gram = (count * count // 128, 128)
    copies = ITERS * (2 * nr * ng + 3 * nr + 2 * nc + 2 * ng) + nr + nc
    vmem = pl.BlockSpec(memory_space=pltpu.VMEM)
    both = pl.pallas_call(
        functools.partial(kernel, nr, nc, fused),
        out_shape=jax.ShapeDtypeStruct((2,) + rhs.shape, F32),
        in_specs=[
            vmem, vmem, pl.BlockSpec(memory_space=pl.ANY), vmem, vmem,
            pl.BlockSpec(memory_space=pltpu.SMEM),
        ],
        out_specs=vmem,
        scratch_shapes=[
            pltpu.VMEM(design_t.shape, BF16),
            pltpu.SemaphoreType.DMA(()),
            pltpu.VMEM((rows if fused else 8, 4, 128), F32),
            pltpu.VMEM((512, 128), F32),
            pltpu.VMEM((width, width), BF16),
            pltpu.VMEM((width, width), BF16),
            pltpu.VMEM((width, width), BF16),
            pltpu.VMEM((count, width), F32),
            pltpu.VMEM((count, obs), F32),
            pltpu.VMEM((ITERS, nr, count, piece), BF16),
            pltpu.VMEM((ITERS, ng, 2, nr, count, piece), BF16),
            pltpu.VMEM((ITERS, nr, count, obs), BF16),
            pltpu.VMEM((ITERS, ng, count, width), F32),
            pltpu.VMEM((ITERS, ng, count, width), F32),
            pltpu.VMEM((ITERS, ng, nr, count, piece), BF16),
            pltpu.VMEM((ITERS, ng, nr, count, piece), BF16),
            pltpu.VMEM((ITERS, nr) + gram, F32),
            pltpu.VMEM((ITERS, nc) + gram, F32),
            pltpu.VMEM((ITERS, nr) + gram, F32),
            pltpu.VMEM((ITERS, nc) + gram, F32),
            pltpu.SemaphoreType.DMA((copies,)),
            pltpu.SemaphoreType.DMA((copies,)),
        ],
        compiler_params=pltpu.CompilerParams(
            collective_id=0, has_side_effects=True, vmem_limit_bytes=60 * 1024 * 1024
        ),
    )(rhs, precond, design_g, terrain.reshape(1, width), order_slot.reshape(1, width), source)
    return pl.pallas_call(
        part_kernel,
        out_shape=(jax.ShapeDtypeStruct(rhs.shape, F32), jax.ShapeDtypeStruct(rhs.shape, F32)),
        in_specs=[vmem],
        out_specs=(vmem, vmem),
    )(both)


def solution(mesh):
    return jax.shard_map(
        on_device,
        mesh=mesh,
        in_specs=(
            P(None, ("row", "col")),
            P(("row", "col"), None, None),
            P("row", "col"),
            P(("row", "col")),
            P(("row", "col")),
            P("row"),
        ),
        out_specs=(P(None, ("row", "col")), P(None, ("row", "col"))),
        check_vma=False,
    )
```

```python
import functools

import jax
import jax.numpy as jnp
from jax import lax
from jax.experimental import pallas as pl
from jax.experimental.pallas import tpu as pltpu
from jax.sharding import PartitionSpec as P

ITERS = 3
PLACED = 6
F32 = jnp.float32
BF16 = jnp.bfloat16
HIGH = lax.Precision.HIGHEST
NT = (((1,), (1,)), ((), ()))
NN = (((1,), (0,)), ((), ()))


def dot(a, b, dims=NN, precision=None):
    return lax.dot_general(a, b, dims, precision=precision, preferred_element_type=F32)


def split(x):
    hi = x.astype(BF16)
    return hi, (x - hi.astype(F32)).astype(BF16)


def pack(gram):
    count = gram.shape[0]
    rows = count * count // 128
    return jnp.concatenate([gram[i * rows : (i + 1) * rows] for i in range(count // rows)], axis=1)


def unpack(packed, count):
    return jnp.concatenate(
        [packed[:, i * count : (i + 1) * count] for i in range(packed.shape[1] // count)], axis=0
    )


def inverses(mats):
    count = mats[0].shape[0]
    eye = (
        lax.broadcasted_iota(jnp.int32, (count, count), 0)
        == lax.broadcasted_iota(jnp.int32, (count, count), 1)
    )
    eye = jnp.where(eye, 1.0, 0.0).astype(F32)
    rows = lax.broadcasted_iota(jnp.int32, (count, 2 * count), 0)
    work = [jnp.concatenate([m, eye], axis=1) for m in mats]
    for k in range(count):
        nxt = []
        for m in work:
            row = m[k : k + 1, :] / m[k : k + 1, k : k + 1]
            nxt.append(jnp.where(rows == k, row, m - m[:, k : k + 1] * row))
        work = nxt
    return [m[:, count:] for m in work]


def kernel(
    nr, nc, fused, rhs, precond, design_hbm, terrain, slot, source, out, design, design_sem,
    stage, ring, pbuf, pbuf_sem, phi, plo, qt, direction, seen,
    arr, wbuf, obuf, psend, precv, zsend, zrecv,
    tbuf, cbuf, grow, gcol, send_sem, recv_sem,
):
    count, width = rhs.shape
    piece = width // nr
    ng = nc // 2
    r = lax.axis_index("row")
    c = lax.axis_index("col")
    g = c // 2
    core = c % 2
    used = [0]
    sent = []

    def send(src, dst, row, col):
        i = used[0]
        used[0] += 1
        copy = pltpu.make_async_remote_copy(
            src_ref=src, dst_ref=dst, send_sem=send_sem.at[i], recv_sem=recv_sem.at[i],
            device_id=(row, col), device_id_type=pl.DeviceIdType.MESH,
        )
        copy.start()
        sent.append(copy)
        return copy

    step_rows = 128

    def chunk_copy(i):
        at = pl.ds(pl.multiple_of(i * step_rows, step_rows), step_rows)
        return pltpu.make_async_copy(precond.at[0, at], pbuf.at[at], pbuf_sem.at[i])

    for i in range(width // step_rows):
        chunk_copy(i).start()
    fetch = pltpu.make_async_copy(design_hbm, design, design_sem)
    fetch.start()
    sol, res = out.at[0], out.at[1]
    barrier = pltpu.get_barrier_semaphore()
    peers = [
        ((r + i) % nr, ((g + d) % ng) * 2 + core) for i in range(nr) for d in range(ng) if i or d
    ] + [(r, ((g + d) % ng) * 2 + 1 - core) for d in range(ng)]
    for peer in peers:
        pl.semaphore_signal(barrier, inc=1, device_id=peer, device_id_type=pl.DeviceIdType.MESH)

    @pl.loop(0, width // step_rows)
    def _(i):
        at = pl.ds(pl.multiple_of(i * step_rows, step_rows), step_rows)
        ids = lax.broadcasted_iota(jnp.int32, (step_rows, width), 0) + i * step_rows
        qt[at, :] = jnp.where(ids == slot[...], 1.0, 0.0).astype(BF16)

    @pl.loop(0, width // step_rows)
    def _(i):
        at = pl.ds(pl.multiple_of(i * step_rows, step_rows), step_rows)
        chunk_copy(i).wait()
        hi, lo = split(pbuf[at, :])
        phi[at, :] = hi
        plo[at, :] = lo

    def precondition(v):
        hi, lo = split(v)
        both = dot(jnp.concatenate([hi, lo], axis=0), phi[...])
        return both[:count] + both[count:] + dot(hi, plo[...])

    def gram(a, b):
        prod = dot(jnp.concatenate(a, axis=0), jnp.concatenate(b, axis=0), NT)
        rows = prod[:count]
        for i in range(1, len(a)):
            rows = rows + prod[i * count : (i + 1) * count]
        total = rows[:, :count]
        for i in range(1, len(b)):
            total = total + rows[:, i * count : (i + 1) * count]
        return total

    def sym_gram(a, b):
        return 0.5 * (gram(a, b) + gram(b, a))

    def rows_out(buf, packed):
        buf[r] = packed.astype(buf.dtype)
        return [send(buf.at[r], buf.at[r], (r + d) % nr, c) for d in range(1, nr)]

    def cols_out(buf, packed):
        buf[c] = packed
        return [send(buf.at[c], buf.at[c], r, (c + d) % nc) for d in range(1, nc)]

    def collect(copies, buf, n):
        for copy in copies:
            copy.wait_recv()
        total = buf[0].astype(F32)
        for i in range(1, n):
            total = total + buf[i].astype(F32)
        return total

    def block(col):
        return design[pl.ds(pl.multiple_of(col * width, width), width), :]

    rows, obs = design.shape
    lanes = obs // 128
    group = ring.shape[0] // 4

    def fill():
        chunk = 512

        @pl.loop(0, rows // chunk)
        def _(i):
            at = pl.multiple_of(i * chunk, chunk)
            for j in range(lanes):
                part = design[pl.ds(at, chunk), j * 128 : (j + 1) * 128].astype(F32)
                stage[pl.ds(at * 4 + j, chunk, stride=4), :] = part

    def place(begin, end):
        @pl.loop(begin, end)
        def _(i):
            at = pl.multiple_of(i * group, group)
            for k in range(group):
                ring[4 * k : 4 * k + 4, :] = stage[pl.ds(source[at + k], 4), :]
            for j in range(lanes):
                part = ring[pl.ds(j, group, stride=4), :]
                design[pl.ds(at, group), j * 128 : (j + 1) * 128] = part.astype(BF16)

    residual = rhs[...]
    precon = precondition(residual)
    sol[...] = jnp.zeros_like(rhs)
    res[...] = residual
    pl.semaphore_wait(barrier, len(peers))
    gamma = gamma_inv = None

    for it in range(ITERS):
        arranged = dot(precon.astype(BF16), qt[...], NT).astype(BF16)
        for i in range(nr):
            arr[it, i] = arranged[:, i * piece : (i + 1) * piece]
        mine = wbuf.at[it, 0, 0]
        mine[r] = arr[it, r]
        order = list(range(1, ng)) + [0]
        moves = {d: [] for d in order}
        for d in order:
            for i in range(nr):
                if i or d:
                    to = (r + i) % nr
                    there = ((g + d) % ng) * 2 + core
                    moves[d].append(send(arr.at[it, to], wbuf.at[it, d, 0, r], to, there))
        gamma_rows = rows_out(grow.at[it], pack(sym_gram(split(precon), split(residual))))

        def terrain_out():
            scaled = terrain[...] * direction[...]
            return rows_out(tbuf.at[it], pack(gram(split(direction[...]), split(scaled))))

        if it == 0:
            direction[...] = precon
            terrain_rows = terrain_out()
            fetch.wait()
            if fused:
                fill()
                place(0, rows // group * PLACED // 8)
        near = []

        def near_out(d):
            for copy in moves[d]:
                copy.wait_recv()
            near.append(send(wbuf.at[it, d, 0], wbuf.at[it, d, 1], r, g * 2 + 1 - core))

        if it == 0 and fused:
            for d in range(ng):
                near_out(d)
            place(rows // group * PLACED // 8, rows // group)
        else:
            near_out(0)

        def product(d, k):
            lhs = jnp.concatenate([wbuf[it, d, k, i] for i in range(nr)], axis=1)
            return dot(lhs, block(((g + ng - d) % ng) * 2 + (core + k) % 2))

        partial = product(0, 0)
        for d in range(1, ng):
            if len(near) == d:
                near_out(d)
            partial = partial + product(d, 0)
            if d == ng // 2:
                gamma_cols = cols_out(gcol.at[it], collect(gamma_rows, grow.at[it], nr))
        for d in range(ng):
            near[d].wait_recv()
            partial = partial + product(d, 1)

        observed_rows = rows_out(obuf.at[it], partial)
        if it:
            gamma = unpack(collect(gamma_cols, gcol.at[it], nc), count)
            beta_t = dot(gamma, gamma_inv, NN, HIGH)
            direction[...] = precon + dot(beta_t, direction[...], NN, HIGH)
            terrain_rows = terrain_out()
            carried = dot(beta_t, seen[...], NN, HIGH)
        observed = collect(observed_rows, obuf.at[it], nr)
        if it:
            observed = observed + carried
        if it + 1 < ITERS:
            seen[...] = observed
        rounded = observed.astype(BF16)
        pairs = [None] * ng

        def pair_out(d):
            psend[it, d] = dot(rounded, block(((g + d) % ng) * 2 + 1 - core), NT)
            pairs[d] = send(psend.at[it, d], precv.at[it, d], r, g * 2 + 1 - core)

        for d in order[:2]:
            pair_out(d)
        curve = sym_gram(split(observed), (rounded,))
        curve = curve + unpack(collect(terrain_rows, tbuf.at[it], nr), count)
        curve_cols = cols_out(cbuf.at[it], pack(curve))
        zs = []
        for n, d in enumerate(order):
            own = dot(rounded, block(((g + d) % ng) * 2 + core), NT)
            if n + 2 < ng:
                pair_out(order[n + 2])
            pairs[d].wait_recv()
            own = own + precv[it, d]
            for i in range(nr):
                zsend[it, d, i] = own[:, i * piece : (i + 1) * piece].astype(BF16)
            for i in range(nr):
                if i or d:
                    to = (r + i) % nr
                    there = ((g + d) % ng) * 2 + core
                    zs.append(send(zsend.at[it, d, to], zrecv.at[it, d, r], to, there))
        zrecv[it, 0, r] = zsend[it, 0, r]
        if it == 0:
            gamma = unpack(collect(gamma_cols, gcol.at[0], nc), count)
        curve = unpack(collect(curve_cols, cbuf.at[it], nc), count)
        if it + 1 < ITERS:
            curve_inv, gamma_inv = inverses([curve, gamma])
        else:
            (curve_inv,) = inverses([curve])
        alpha_t = dot(gamma, curve_inv, NN, HIGH)
        sol[...] += dot(alpha_t, direction[...], NN, HIGH)
        for copy in zs:
            copy.wait_recv()
        pieces = []
        for i in range(nr):
            total = zrecv[it, 0, i].astype(F32)
            for d in range(1, ng):
                total = total + zrecv[it, d, i].astype(F32)
            pieces.append(total)
        arrived = jnp.concatenate(pieces, axis=1)
        both = dot(jnp.concatenate(split(arrived), axis=0), qt[...])
        image = both[:count] + both[count:] + terrain[...] * direction[...]
        residual = res[...] - dot(alpha_t, image, NN, HIGH)
        res[...] = residual
        if it + 1 < ITERS:
            precon = precondition(residual)

    for copy in sent:
        copy.wait_send()


def part_kernel(both, sol, res):
    sol[...] = both[0]
    res[...] = both[1]


def bits(n):
    assert n & (n - 1) == 0
    return n.bit_length() - 1


def source_kernel(nr, nc, piece, wanted, out):
    rows = wanted.shape[1]
    high = rows // 128
    chunk = 1024

    def step(i, total):
        w = wanted[:, i * chunk : (i + 1) * chunk]
        owner = w >> bits(piece)
        pos = ((owner & (nc - 1)) * nr + (owner >> bits(nc))) * piece + (w & (piece - 1))
        here = lax.broadcasted_iota(jnp.int32, (high, chunk), 1) + i * chunk
        hit = lax.broadcasted_iota(jnp.int32, (high, chunk), 0) == (pos >> 7)
        upper = jnp.where(hit, (here >> 7).astype(F32), 0.0)
        lower = jnp.where(hit, (here & 127).astype(F32), 0.0)
        lhs = jnp.concatenate([upper, lower], axis=0).astype(BF16)
        lane = lax.broadcasted_iota(jnp.int32, (128, chunk), 0) == (pos & 127)
        return total + dot(lhs, jnp.where(lane, 1.0, 0.0).astype(BF16), NT)

    total = jnp.zeros((2 * high, 128), F32)
    for i in range(rows // chunk):
        total = step(i, total)
    out[...] = (512.0 * total[:high] + 4.0 * total[high:]).astype(jnp.int32)


def source_rows(degree_source, nr, nc, piece):
    rows = degree_source.shape[0]
    vmem = pl.BlockSpec(memory_space=pltpu.VMEM)
    return pl.pallas_call(
        functools.partial(source_kernel, nr, nc, piece),
        out_shape=jax.ShapeDtypeStruct((rows // 128, 128), jnp.int32),
        in_specs=[vmem],
        out_specs=vmem,
    )(degree_source.reshape(1, rows)).reshape(rows)


def place_kernel(steps, chunk, lanes, pos, design, out, stage, placed):
    i = pl.program_id(0)

    @pl.when(i < steps)
    def _():
        for j in range(lanes):
            stage[pl.ds(j, chunk, stride=4), :] = design[:, j * 128 : (j + 1) * 128].astype(F32)
        base = i * chunk

        @pl.loop(0, chunk // 64)
        def _(n):
            for k in range(64):
                row = n * 64 + k
                to = pl.multiple_of(pos[base + row], 4)
                placed[pl.ds(to, 4), :] = stage[pl.ds(pl.multiple_of(row * 4, 4), 4), :]

    @pl.when(i >= steps)
    def _():
        base = pl.multiple_of((i - steps) * (chunk * 4), chunk * 4)
        for j in range(lanes):
            out[:, j * 128 : (j + 1) * 128] = placed[pl.ds(base + j, chunk, stride=4), :].astype(BF16)


def place_rows(design_t, pos):
    rows, obs = design_t.shape
    chunk = 512
    steps = rows // chunk
    return pl.pallas_call(
        functools.partial(place_kernel, steps, chunk, obs // 128),
        grid=(2 * steps,),
        out_shape=jax.ShapeDtypeStruct(design_t.shape, design_t.dtype),
        in_specs=[
            pl.BlockSpec(memory_space=pltpu.SMEM),
            pl.BlockSpec((chunk, obs), lambda i: (jnp.minimum(i, steps - 1), 0)),
        ],
        out_specs=pl.BlockSpec((chunk, obs), lambda i: (jnp.maximum(i - steps, 0), 0)),
        scratch_shapes=[pltpu.VMEM((4 * chunk, 128), F32), pltpu.VMEM((4 * rows, 128), F32)],
        compiler_params=pltpu.CompilerParams(vmem_limit_bytes=48 * 1024 * 1024),
    )(4 * pos, design_t)


def on_device(rhs, precond, design_t, terrain, order_slot, degree_source):
    nr = lax.axis_size("row")
    nc = lax.axis_size("col")
    count, width = rhs.shape
    piece = width // nr
    ng = nc // 2
    obs = design_t.shape[1]
    rows = design_t.shape[0]
    fused = rows <= 8192
    if fused:
        design_g = design_t
        source = source_rows(degree_source, nr, nc, piece)
    else:
        owner = degree_source // piece
        within = degree_source % piece
        design_g = place_rows(design_t, (owner % nc * nr + owner // nc) * piece + within)
        source = degree_source[:128]
    gram = (count * count // 128, 128)
    copies = ITERS * (2 * nr * ng + 3 * nr + 2 * nc + 2 * ng) + nr + nc
    vmem = pl.BlockSpec(memory_space=pltpu.VMEM)
    both = pl.pallas_call(
        functools.partial(kernel, nr, nc, fused),
        out_shape=jax.ShapeDtypeStruct((2,) + rhs.shape, F32),
        in_specs=[
            vmem, pl.BlockSpec(memory_space=pl.ANY), pl.BlockSpec(memory_space=pl.ANY), vmem, vmem,
            pl.BlockSpec(memory_space=pltpu.SMEM),
        ],
        out_specs=vmem,
        scratch_shapes=[
            pltpu.VMEM(design_t.shape, BF16),
            pltpu.SemaphoreType.DMA(()),
            pltpu.VMEM((4 * rows if fused else 8, 128), F32),
            pltpu.VMEM((512, 128), F32),
            pltpu.VMEM((width, width), F32),
            pltpu.SemaphoreType.DMA((width // 128,)),
            pltpu.VMEM((width, width), BF16),
            pltpu.VMEM((width, width), BF16),
            pltpu.VMEM((width, width), BF16),
            pltpu.VMEM((count, width), F32),
            pltpu.VMEM((count, obs), F32),
            pltpu.VMEM((ITERS, nr, count, piece), BF16),
            pltpu.VMEM((ITERS, ng, 2, nr, count, piece), BF16),
            pltpu.VMEM((ITERS, nr, count, obs), BF16),
            pltpu.VMEM((ITERS, ng, count, width), F32),
            pltpu.VMEM((ITERS, ng, count, width), F32),
            pltpu.VMEM((ITERS, ng, nr, count, piece), BF16),
            pltpu.VMEM((ITERS, ng, nr, count, piece), BF16),
            pltpu.VMEM((ITERS, nr) + gram, F32),
            pltpu.VMEM((ITERS, nc) + gram, F32),
            pltpu.VMEM((ITERS, nr) + gram, F32),
            pltpu.VMEM((ITERS, nc) + gram, F32),
            pltpu.SemaphoreType.DMA((copies,)),
            pltpu.SemaphoreType.DMA((copies,)),
        ],
        compiler_params=pltpu.CompilerParams(
            collective_id=0, has_side_effects=True, vmem_limit_bytes=60 * 1024 * 1024
        ),
    )(rhs, precond, design_g, terrain.reshape(1, width), order_slot.reshape(1, width), source)
    return pl.pallas_call(
        part_kernel,
        out_shape=(jax.ShapeDtypeStruct(rhs.shape, F32), jax.ShapeDtypeStruct(rhs.shape, F32)),
        in_specs=[vmem],
        out_specs=(vmem, vmem),
    )(both)


def solution(mesh):
    return jax.shard_map(
        on_device,
        mesh=mesh,
        in_specs=(
            P(None, ("row", "col")),
            P(("row", "col"), None, None),
            P("row", "col"),
            P(("row", "col")),
            P(("row", "col")),
            P("row"),
        ),
        out_specs=(P(None, ("row", "col")), P(None, ("row", "col"))),
        check_vma=False,
    )
```

```python
import functools

import jax
import jax.numpy as jnp
from jax import lax
from jax.experimental import pallas as pl
from jax.experimental.pallas import tpu as pltpu
from jax.sharding import PartitionSpec as P

ITERS = 3
PLACED = 7
F32 = jnp.float32
BF16 = jnp.bfloat16
HIGH = lax.Precision.HIGHEST
NT = (((1,), (1,)), ((), ()))
NN = (((1,), (0,)), ((), ()))


def dot(a, b, dims=NN, precision=None):
    return lax.dot_general(a, b, dims, precision=precision, preferred_element_type=F32)


def split(x):
    hi = x.astype(BF16)
    return hi, (x - hi.astype(F32)).astype(BF16)


def pack(gram):
    count = gram.shape[0]
    rows = count * count // 128
    return jnp.concatenate([gram[i * rows : (i + 1) * rows] for i in range(count // rows)], axis=1)


def unpack(packed, count):
    return jnp.concatenate(
        [packed[:, i * count : (i + 1) * count] for i in range(packed.shape[1] // count)], axis=0
    )


def inverses(mats):
    count = mats[0].shape[0]
    eye = (
        lax.broadcasted_iota(jnp.int32, (count, count), 0)
        == lax.broadcasted_iota(jnp.int32, (count, count), 1)
    )
    eye = jnp.where(eye, 1.0, 0.0).astype(F32)
    rows = lax.broadcasted_iota(jnp.int32, (count, 2 * count), 0)
    work = [jnp.concatenate([m, eye], axis=1) for m in mats]
    for k in range(count):
        nxt = []
        for m in work:
            row = m[k : k + 1, :] / m[k : k + 1, k : k + 1]
            nxt.append(jnp.where(rows == k, row, m - m[:, k : k + 1] * row))
        work = nxt
    return [m[:, count:] for m in work]


def bits(n):
    assert n & (n - 1) == 0
    return n.bit_length() - 1


def kernel(
    nr, nc, fused, rhs, precond, design_hbm, terrain, slot, source, out, design, design_sem,
    stage, ring, pbuf, pbuf_sem, phi, plo, qt, direction, seen,
    arr, wbuf, obuf, psend, precv, zsend, zrecv,
    tbuf, cbuf, grow, gcol, send_sem, recv_sem,
):
    count, width = rhs.shape
    piece = width // nr
    ng = nc // 2
    r = lax.axis_index("row")
    c = lax.axis_index("col")
    g = c // 2
    core = c % 2
    used = [0]
    sent = []

    far = []
    for d in range(ng):
        at = g
        for k in range(bits(ng)):
            if d >> k & 1:
                at = at + 2**k - 2 ** (k + 1) * (at // 2**k % 2)
        far.append(at)
    order = []
    for k in reversed(range(bits(ng))):
        order += range(2**k, 2 ** (k + 1))
    order.append(0)

    def send(src, dst, row, col):
        i = used[0]
        used[0] += 1
        copy = pltpu.make_async_remote_copy(
            src_ref=src, dst_ref=dst, send_sem=send_sem.at[i], recv_sem=recv_sem.at[i],
            device_id=(row, col), device_id_type=pl.DeviceIdType.MESH,
        )
        copy.start()
        sent.append(copy)
        return copy

    step_rows = 128

    def chunk_copy(i):
        at = pl.ds(pl.multiple_of(i * step_rows, step_rows), step_rows)
        return pltpu.make_async_copy(precond.at[0, at], pbuf.at[at], pbuf_sem.at[i])

    for i in range(width // step_rows):
        chunk_copy(i).start()
    fetch = pltpu.make_async_copy(design_hbm, design, design_sem)
    fetch.start()
    sol, res = out.at[0], out.at[1]
    barrier = pltpu.get_barrier_semaphore()
    peers = [
        ((r + i) % nr, ((g + d) % ng) * 2 + core) for i in range(nr) for d in range(ng) if i or d
    ] + [(r, ((g + d) % ng) * 2 + 1 - core) for d in range(ng)]
    for peer in peers:
        pl.semaphore_signal(barrier, inc=1, device_id=peer, device_id_type=pl.DeviceIdType.MESH)

    @pl.loop(0, width // step_rows)
    def _(i):
        at = pl.ds(pl.multiple_of(i * step_rows, step_rows), step_rows)
        ids = lax.broadcasted_iota(jnp.int32, (step_rows, width), 0) + i * step_rows
        qt[at, :] = jnp.where(ids == slot[...], 1.0, 0.0).astype(BF16)

    @pl.loop(0, width // step_rows)
    def _(i):
        at = pl.ds(pl.multiple_of(i * step_rows, step_rows), step_rows)
        chunk_copy(i).wait()
        hi, lo = split(pbuf[at, :])
        phi[at, :] = hi
        plo[at, :] = lo

    def precondition(v):
        hi, lo = split(v)
        both = dot(jnp.concatenate([hi, lo], axis=0), phi[...])
        return both[:count] + both[count:] + dot(hi, plo[...])

    def gram(a, b):
        prod = dot(jnp.concatenate(a, axis=0), jnp.concatenate(b, axis=0), NT)
        rows = prod[:count]
        for i in range(1, len(a)):
            rows = rows + prod[i * count : (i + 1) * count]
        total = rows[:, :count]
        for i in range(1, len(b)):
            total = total + rows[:, i * count : (i + 1) * count]
        return total

    def sym_gram(a, b):
        return 0.5 * (gram(a, b) + gram(b, a))

    def rows_out(buf, packed):
        buf[r] = packed.astype(buf.dtype)
        return [send(buf.at[r], buf.at[r], (r + d) % nr, c) for d in range(1, nr)]

    def cols_out(buf, packed):
        buf[c] = packed
        return [send(buf.at[c], buf.at[c], r, (c + d) % nc) for d in range(1, nc)]

    def collect(copies, buf, n):
        for copy in copies:
            copy.wait_recv()
        total = buf[0].astype(F32)
        for i in range(1, n):
            total = total + buf[i].astype(F32)
        return total

    def block(col):
        return design[pl.ds(pl.multiple_of(col * width, width), width), :]

    rows, obs = design.shape
    lanes = obs // 128
    group = ring.shape[0] // 4

    def fill():
        chunk = 512

        @pl.loop(0, rows // chunk)
        def _(i):
            at = pl.multiple_of(i * chunk, chunk)
            for j in range(lanes):
                part = design[pl.ds(at, chunk), j * 128 : (j + 1) * 128].astype(F32)
                stage[pl.ds(at * 4 + j, chunk, stride=4), :] = part

    def place(begin, end):
        @pl.loop(begin, end)
        def _(i):
            at = pl.multiple_of(i * group, group)
            for k in range(group):
                ring[4 * k : 4 * k + 4, :] = stage[pl.ds(source[at + k], 4), :]
            for j in range(lanes):
                part = ring[pl.ds(j, group, stride=4), :]
                design[pl.ds(at, group), j * 128 : (j + 1) * 128] = part.astype(BF16)

    residual = rhs[...]
    precon = precondition(residual)
    sol[...] = jnp.zeros_like(rhs)
    res[...] = residual
    pl.semaphore_wait(barrier, len(peers))
    gamma = gamma_inv = None

    for it in range(ITERS):
        lowered = precon.astype(BF16)
        moves = {d: [] for d in order}
        for i in range(nr):
            to = (r + i) % nr
            picks = qt[pl.ds(pl.multiple_of(to * piece, piece), piece), :]
            arr[it, i] = dot(lowered, picks, NT).astype(BF16)
            for d in order:
                if i or d:
                    there = far[d] * 2 + core
                    moves[d].append(send(arr.at[it, i], wbuf.at[it, d, 0, r], to, there))
        mine = wbuf.at[it, 0, 0]
        mine[r] = arr[it, 0]
        gamma_rows = rows_out(grow.at[it], pack(sym_gram(split(precon), split(residual))))

        def terrain_out():
            scaled = terrain[...] * direction[...]
            return rows_out(tbuf.at[it], pack(gram(split(direction[...]), split(scaled))))

        if it == 0:
            direction[...] = precon
            terrain_rows = terrain_out()
            fetch.wait()
            if fused:
                fill()
                place(0, rows // group * PLACED // 8)
        near = []

        def near_out(d):
            for copy in moves[d]:
                copy.wait_recv()
            near.append(send(wbuf.at[it, d, 0], wbuf.at[it, d, 1], r, g * 2 + 1 - core))

        if it == 0 and fused:
            for d in range(ng):
                near_out(d)
            place(rows // group * PLACED // 8, rows // group)
        else:
            near_out(0)

        def product(d, k):
            lhs = jnp.concatenate([wbuf[it, d, k, i] for i in range(nr)], axis=1)
            return dot(lhs, block(far[d] * 2 + (core + k) % 2))

        partial = product(0, 0)
        for d in range(1, ng):
            if len(near) == d:
                near_out(d)
            partial = partial + product(d, 0)
            if d == ng // 2:
                gamma_cols = cols_out(gcol.at[it], collect(gamma_rows, grow.at[it], nr))
        for d in range(ng):
            near[d].wait_recv()
            partial = partial + product(d, 1)

        observed_rows = rows_out(obuf.at[it], partial)
        if it:
            gamma = unpack(collect(gamma_cols, gcol.at[it], nc), count)
            beta_t = dot(gamma, gamma_inv, NN, HIGH)
            direction[...] = precon + dot(beta_t, direction[...], NN, HIGH)
            terrain_rows = terrain_out()
            carried = dot(beta_t, seen[...], NN, HIGH)
        observed = collect(observed_rows, obuf.at[it], nr)
        if it:
            observed = observed + carried
        if it + 1 < ITERS:
            seen[...] = observed
        rounded = observed.astype(BF16)
        pairs = [None] * ng

        def pair_out(d):
            psend[it, d] = dot(rounded, block(far[d] * 2 + 1 - core), NT)
            pairs[d] = send(psend.at[it, d], precv.at[it, d], r, g * 2 + 1 - core)

        for d in order[:2]:
            pair_out(d)
        curve = sym_gram(split(observed), (rounded,))
        curve = curve + unpack(collect(terrain_rows, tbuf.at[it], nr), count)
        curve_cols = cols_out(cbuf.at[it], pack(curve))
        zs = []
        for n, d in enumerate(order):
            own = dot(rounded, block(far[d] * 2 + core), NT)
            if n + 2 < ng:
                pair_out(order[n + 2])
            pairs[d].wait_recv()
            own = own + precv[it, d]
            for i in range(nr):
                zsend[it, d, i] = own[:, i * piece : (i + 1) * piece].astype(BF16)
            for i in range(nr):
                if i or d:
                    to = (r + i) % nr
                    there = far[d] * 2 + core
                    zs.append(send(zsend.at[it, d, to], zrecv.at[it, d, r], to, there))
        zrecv[it, 0, r] = zsend[it, 0, r]
        if it == 0:
            gamma = unpack(collect(gamma_cols, gcol.at[0], nc), count)
        curve = unpack(collect(curve_cols, cbuf.at[it], nc), count)
        if it + 1 < ITERS:
            curve_inv, gamma_inv = inverses([curve, gamma])
        else:
            (curve_inv,) = inverses([curve])
        alpha_t = dot(gamma, curve_inv, NN, HIGH)
        sol[...] += dot(alpha_t, direction[...], NN, HIGH)
        alpha_both = jnp.concatenate(split(alpha_t), axis=0)
        for copy in zs:
            copy.wait_recv()
        pieces = []
        for i in range(nr):
            total = zrecv[it, 0, i].astype(F32)
            for d in range(1, ng):
                total = total + zrecv[it, d, i].astype(F32)
            pieces.append(total)
        arrived = jnp.concatenate(pieces, axis=1)
        both = dot(jnp.concatenate(split(arrived), axis=0), qt[...])
        image = both[:count] + both[count:] + terrain[...] * direction[...]
        image_hi, image_lo = split(image)
        steps = dot(alpha_both, image_hi)
        residual = res[...] - (steps[:count] + steps[count:] + dot(alpha_both[:count], image_lo))
        res[...] = residual
        if it + 1 < ITERS:
            precon = precondition(residual)

    for copy in sent:
        copy.wait_send()


def part_kernel(both, sol, res):
    sol[...] = both[0]
    res[...] = both[1]


def source_kernel(nr, nc, piece, wanted, out):
    rows = wanted.shape[1]
    high = rows // 128
    chunk = 1024

    def step(i, total):
        w = wanted[:, i * chunk : (i + 1) * chunk]
        owner = w >> bits(piece)
        pos = ((owner & (nc - 1)) * nr + (owner >> bits(nc))) * piece + (w & (piece - 1))
        here = lax.broadcasted_iota(jnp.int32, (high, chunk), 1) + i * chunk
        hit = lax.broadcasted_iota(jnp.int32, (high, chunk), 0) == (pos >> 7)
        upper = jnp.where(hit, (here >> 7).astype(F32), 0.0)
        lower = jnp.where(hit, (here & 127).astype(F32), 0.0)
        lhs = jnp.concatenate([upper, lower], axis=0).astype(BF16)
        lane = lax.broadcasted_iota(jnp.int32, (128, chunk), 0) == (pos & 127)
        return total + dot(lhs, jnp.where(lane, 1.0, 0.0).astype(BF16), NT)

    total = jnp.zeros((2 * high, 128), F32)
    for i in range(rows // chunk):
        total = step(i, total)
    out[...] = (512.0 * total[:high] + 4.0 * total[high:]).astype(jnp.int32)


def source_rows(degree_source, nr, nc, piece):
    rows = degree_source.shape[0]
    vmem = pl.BlockSpec(memory_space=pltpu.VMEM)
    return pl.pallas_call(
        functools.partial(source_kernel, nr, nc, piece),
        out_shape=jax.ShapeDtypeStruct((rows // 128, 128), jnp.int32),
        in_specs=[vmem],
        out_specs=vmem,
    )(degree_source.reshape(1, rows)).reshape(rows)


def place_kernel(steps, chunk, lanes, pos, design, out, stage, placed):
    i = pl.program_id(0)

    @pl.when(i < steps)
    def _():
        for j in range(lanes):
            stage[pl.ds(j, chunk, stride=4), :] = design[:, j * 128 : (j + 1) * 128].astype(F32)
        base = i * chunk

        @pl.loop(0, chunk // 64)
        def _(n):
            for k in range(64):
                row = n * 64 + k
                to = pl.multiple_of(pos[base + row], 4)
                placed[pl.ds(to, 4), :] = stage[pl.ds(pl.multiple_of(row * 4, 4), 4), :]

    @pl.when(i >= steps)
    def _():
        base = pl.multiple_of((i - steps) * (chunk * 4), chunk * 4)
        for j in range(lanes):
            out[:, j * 128 : (j + 1) * 128] = placed[pl.ds(base + j, chunk, stride=4), :].astype(BF16)


def place_rows(design_t, pos):
    rows, obs = design_t.shape
    chunk = 512
    steps = rows // chunk
    return pl.pallas_call(
        functools.partial(place_kernel, steps, chunk, obs // 128),
        grid=(2 * steps,),
        out_shape=jax.ShapeDtypeStruct(design_t.shape, design_t.dtype),
        in_specs=[
            pl.BlockSpec(memory_space=pltpu.SMEM),
            pl.BlockSpec((chunk, obs), lambda i: (jnp.minimum(i, steps - 1), 0)),
        ],
        out_specs=pl.BlockSpec((chunk, obs), lambda i: (jnp.maximum(i - steps, 0), 0)),
        scratch_shapes=[pltpu.VMEM((4 * chunk, 128), F32), pltpu.VMEM((4 * rows, 128), F32)],
        compiler_params=pltpu.CompilerParams(vmem_limit_bytes=48 * 1024 * 1024),
    )(4 * pos, design_t)


def on_device(rhs, precond, design_t, terrain, order_slot, degree_source):
    nr = lax.axis_size("row")
    nc = lax.axis_size("col")
    count, width = rhs.shape
    piece = width // nr
    ng = nc // 2
    obs = design_t.shape[1]
    rows = design_t.shape[0]
    fused = rows <= 8192
    if fused:
        design_g = design_t
        source = source_rows(degree_source, nr, nc, piece)
    else:
        owner = degree_source // piece
        within = degree_source % piece
        design_g = place_rows(design_t, (owner % nc * nr + owner // nc) * piece + within)
        source = degree_source[:128]
    gram = (count * count // 128, 128)
    copies = ITERS * (2 * nr * ng + 3 * nr + 2 * nc + 2 * ng) + nr + nc
    vmem = pl.BlockSpec(memory_space=pltpu.VMEM)
    both = pl.pallas_call(
        functools.partial(kernel, nr, nc, fused),
        out_shape=jax.ShapeDtypeStruct((2,) + rhs.shape, F32),
        in_specs=[
            vmem, pl.BlockSpec(memory_space=pl.ANY), pl.BlockSpec(memory_space=pl.ANY), vmem, vmem,
            pl.BlockSpec(memory_space=pltpu.SMEM),
        ],
        out_specs=vmem,
        scratch_shapes=[
            pltpu.VMEM(design_t.shape, BF16),
            pltpu.SemaphoreType.DMA(()),
            pltpu.VMEM((4 * rows if fused else 8, 128), F32),
            pltpu.VMEM((512, 128), F32),
            pltpu.VMEM((width, width), F32),
            pltpu.SemaphoreType.DMA((width // 128,)),
            pltpu.VMEM((width, width), BF16),
            pltpu.VMEM((width, width), BF16),
            pltpu.VMEM((width, width), BF16),
            pltpu.VMEM((count, width), F32),
            pltpu.VMEM((count, obs), F32),
            pltpu.VMEM((ITERS, nr, count, piece), BF16),
            pltpu.VMEM((ITERS, ng, 2, nr, count, piece), BF16),
            pltpu.VMEM((ITERS, nr, count, obs), BF16),
            pltpu.VMEM((ITERS, ng, count, width), F32),
            pltpu.VMEM((ITERS, ng, count, width), F32),
            pltpu.VMEM((ITERS, ng, nr, count, piece), BF16),
            pltpu.VMEM((ITERS, ng, nr, count, piece), BF16),
            pltpu.VMEM((ITERS, nr) + gram, F32),
            pltpu.VMEM((ITERS, nc) + gram, F32),
            pltpu.VMEM((ITERS, nr) + gram, F32),
            pltpu.VMEM((ITERS, nc) + gram, F32),
            pltpu.SemaphoreType.DMA((copies,)),
            pltpu.SemaphoreType.DMA((copies,)),
        ],
        compiler_params=pltpu.CompilerParams(
            collective_id=0, has_side_effects=True, vmem_limit_bytes=60 * 1024 * 1024
        ),
    )(rhs, precond, design_g, terrain.reshape(1, width), order_slot.reshape(1, width), source)
    return pl.pallas_call(
        part_kernel,
        out_shape=(jax.ShapeDtypeStruct(rhs.shape, F32), jax.ShapeDtypeStruct(rhs.shape, F32)),
        in_specs=[vmem],
        out_specs=(vmem, vmem),
    )(both)


def solution(mesh):
    return jax.shard_map(
        on_device,
        mesh=mesh,
        in_specs=(
            P(None, ("row", "col")),
            P(("row", "col"), None, None),
            P("row", "col"),
            P(("row", "col")),
            P(("row", "col")),
            P("row"),
        ),
        out_specs=(P(None, ("row", "col")), P(None, ("row", "col"))),
        check_vma=False,
    )
```

```python
import functools

import jax
import jax.numpy as jnp
from jax import lax
from jax.experimental import pallas as pl
from jax.experimental.pallas import tpu as pltpu
from jax.sharding import PartitionSpec as P

ITERS = 3
PLACED = 7
F32 = jnp.float32
BF16 = jnp.bfloat16
HIGH = lax.Precision.HIGHEST
NT = (((1,), (1,)), ((), ()))
NN = (((1,), (0,)), ((), ()))


def dot(a, b, dims=NN, precision=None):
    return lax.dot_general(a, b, dims, precision=precision, preferred_element_type=F32)


def split(x):
    hi = x.astype(BF16)
    return hi, (x - hi.astype(F32)).astype(BF16)


def mix(coeff, x):
    count = coeff.shape[0]
    hi, lo = split(x)
    c_hi, c_lo = split(coeff)
    steps = dot(jnp.concatenate([c_hi, c_lo], axis=0), hi)
    return steps[:count] + steps[count:] + dot(c_hi, lo)


def pack(gram):
    count = gram.shape[0]
    rows = count * count // 128
    return jnp.concatenate([gram[i * rows : (i + 1) * rows] for i in range(count // rows)], axis=1)


def unpack(packed, count):
    return jnp.concatenate(
        [packed[:, i * count : (i + 1) * count] for i in range(packed.shape[1] // count)], axis=0
    )


def inverses(mats):
    count = mats[0].shape[0]
    eye = (
        lax.broadcasted_iota(jnp.int32, (count, count), 0)
        == lax.broadcasted_iota(jnp.int32, (count, count), 1)
    )
    eye = jnp.where(eye, 1.0, 0.0).astype(F32)
    rows = lax.broadcasted_iota(jnp.int32, (count, 2 * count), 0)
    work = [jnp.concatenate([m, eye], axis=1) for m in mats]
    for k in range(count):
        nxt = []
        for m in work:
            row = m[k : k + 1, :] / m[k : k + 1, k : k + 1]
            nxt.append(jnp.where(rows == k, row, m - m[:, k : k + 1] * row))
        work = nxt
    return [m[:, count:] for m in work]


def bits(n):
    assert n & (n - 1) == 0
    return n.bit_length() - 1


def kernel(
    nr, nc, fused, rhs, precond, design_hbm, terrain, slot, source, out, design, design_sem,
    stage, ring, pbuf, pbuf_sem, phi, plo, qt, direction, seen,
    arr, wbuf, obuf, psend, precv, zsend, zrecv,
    tbuf, cbuf, grow, gcol, send_sem, recv_sem,
):
    count, width = rhs.shape
    piece = width // nr
    ng = nc // 2
    r = lax.axis_index("row")
    c = lax.axis_index("col")
    g = c // 2
    core = c % 2
    used = [0]
    sent = []

    far = []
    for d in range(ng):
        at = g
        for k in range(bits(ng)):
            if d >> k & 1:
                at = at + 2**k - 2 ** (k + 1) * (at // 2**k % 2)
        far.append(at)
    order = []
    for k in reversed(range(bits(ng))):
        order += range(2**k, 2 ** (k + 1))
    order.append(0)

    def send(src, dst, row, col):
        i = used[0]
        used[0] += 1
        copy = pltpu.make_async_remote_copy(
            src_ref=src, dst_ref=dst, send_sem=send_sem.at[i], recv_sem=recv_sem.at[i],
            device_id=(row, col), device_id_type=pl.DeviceIdType.MESH,
        )
        copy.start()
        sent.append(copy)
        return copy

    step_rows = 128

    def chunk_copy(i):
        at = pl.ds(pl.multiple_of(i * step_rows, step_rows), step_rows)
        return pltpu.make_async_copy(precond.at[0, at], pbuf.at[at], pbuf_sem.at[i])

    for i in range(width // step_rows):
        chunk_copy(i).start()
    fetch = pltpu.make_async_copy(design_hbm, design, design_sem)
    fetch.start()
    sol, res = out.at[0], out.at[1]
    barrier = pltpu.get_barrier_semaphore()
    peers = [
        ((r + i) % nr, ((g + d) % ng) * 2 + core) for i in range(nr) for d in range(ng) if i or d
    ] + [(r, ((g + d) % ng) * 2 + 1 - core) for d in range(ng)]
    for peer in peers:
        pl.semaphore_signal(barrier, inc=1, device_id=peer, device_id_type=pl.DeviceIdType.MESH)

    @pl.loop(0, width // step_rows)
    def _(i):
        at = pl.ds(pl.multiple_of(i * step_rows, step_rows), step_rows)
        ids = lax.broadcasted_iota(jnp.int32, (step_rows, width), 0) + i * step_rows
        qt[at, :] = jnp.where(ids == slot[...], 1.0, 0.0).astype(BF16)

    @pl.loop(0, width // step_rows)
    def _(i):
        at = pl.ds(pl.multiple_of(i * step_rows, step_rows), step_rows)
        chunk_copy(i).wait()
        hi, lo = split(pbuf[at, :])
        phi[at, :] = hi
        plo[at, :] = lo

    def precondition(v):
        hi, lo = split(v)
        both = dot(jnp.concatenate([hi, lo], axis=0), phi[...])
        return both[:count] + both[count:] + dot(hi, plo[...])

    def gram(a, b):
        prod = dot(jnp.concatenate(a, axis=0), jnp.concatenate(b, axis=0), NT)
        rows = prod[:count]
        for i in range(1, len(a)):
            rows = rows + prod[i * count : (i + 1) * count]
        total = rows[:, :count]
        for i in range(1, len(b)):
            total = total + rows[:, i * count : (i + 1) * count]
        return total

    def sym_gram(a, b):
        return 0.5 * (gram(a, b) + gram(b, a))

    def rows_out(buf, packed):
        buf[r] = packed.astype(buf.dtype)
        return [send(buf.at[r], buf.at[r], (r + d) % nr, c) for d in range(1, nr)]

    def cols_out(buf, packed):
        buf[c] = packed
        return [send(buf.at[c], buf.at[c], r, (c + d) % nc) for d in range(1, nc)]

    def collect(copies, buf, n):
        for copy in copies:
            copy.wait_recv()
        total = buf[0].astype(F32)
        for i in range(1, n):
            total = total + buf[i].astype(F32)
        return total

    def block(col):
        return design[pl.ds(pl.multiple_of(col * width, width), width), :]

    rows, obs = design.shape
    lanes = obs // 128
    group = ring.shape[0] // 4

    def fill():
        chunk = 512

        @pl.loop(0, rows // chunk)
        def _(i):
            at = pl.multiple_of(i * chunk, chunk)
            for j in range(lanes):
                part = design[pl.ds(at, chunk), j * 128 : (j + 1) * 128].astype(F32)
                stage[pl.ds(at * 4 + j, chunk, stride=4), :] = part

    def place(begin, end):
        @pl.loop(begin, end)
        def _(i):
            at = pl.multiple_of(i * group, group)
            for k in range(group):
                ring[4 * k : 4 * k + 4, :] = stage[pl.ds(source[at + k], 4), :]
            for j in range(lanes):
                part = ring[pl.ds(j, group, stride=4), :]
                design[pl.ds(at, group), j * 128 : (j + 1) * 128] = part.astype(BF16)

    residual = rhs[...]
    precon = precondition(residual)
    sol[...] = jnp.zeros_like(rhs)
    res[...] = residual
    pl.semaphore_wait(barrier, len(peers))
    gamma = gamma_inv = None

    for it in range(ITERS):
        lowered = precon.astype(BF16)
        moves = {d: [] for d in order}
        for i in range(nr):
            to = (r + i) % nr
            picks = qt[pl.ds(pl.multiple_of(to * piece, piece), piece), :]
            arr[it, i] = dot(lowered, picks, NT).astype(BF16)
            for d in order:
                if i or d:
                    there = far[d] * 2 + core
                    moves[d].append(send(arr.at[it, i], wbuf.at[it, d, 0, r], to, there))
        mine = wbuf.at[it, 0, 0]
        mine[r] = arr[it, 0]
        gamma_rows = rows_out(grow.at[it], pack(sym_gram(split(precon), split(residual))))

        def terrain_out():
            scaled = terrain[...] * direction[...]
            return rows_out(tbuf.at[it], pack(gram(split(direction[...]), split(scaled))))

        if it == 0:
            direction[...] = precon
            terrain_rows = terrain_out()
            fetch.wait()
            if fused:
                fill()
                place(0, rows // group * PLACED // 8)
        near = []

        def near_out(d):
            for copy in moves[d]:
                copy.wait_recv()
            near.append(send(wbuf.at[it, d, 0], wbuf.at[it, d, 1], r, g * 2 + 1 - core))

        if it == 0 and fused:
            for d in range(ng):
                near_out(d)
            place(rows // group * PLACED // 8, rows // group)
        else:
            near_out(0)

        def product(d, k):
            lhs = jnp.concatenate([wbuf[it, d, k, i] for i in range(nr)], axis=1)
            return dot(lhs, block(far[d] * 2 + (core + k) % 2))

        partial = product(0, 0)
        for d in range(1, ng):
            if len(near) == d:
                near_out(d)
            partial = partial + product(d, 0)
            if d == ng // 2 - 1:
                gamma_cols = cols_out(gcol.at[it], collect(gamma_rows, grow.at[it], nr))
        for d in range(ng):
            near[d].wait_recv()
            partial = partial + product(d, 1)

        observed_rows = rows_out(obuf.at[it], partial)
        if it:
            gamma = unpack(collect(gamma_cols, gcol.at[it], nc), count)
            beta_t = dot(gamma, gamma_inv, NN, HIGH)
            direction[...] = precon + mix(beta_t, direction[...])
            terrain_rows = terrain_out()
            carried = mix(beta_t, seen[...])
        observed = collect(observed_rows, obuf.at[it], nr)
        if it:
            observed = observed + carried
        if it + 1 < ITERS:
            seen[...] = observed
        rounded = observed.astype(BF16)
        pairs = [None] * ng

        def pair_out(d):
            psend[it, d] = dot(rounded, block(far[d] * 2 + 1 - core), NT)
            pairs[d] = send(psend.at[it, d], precv.at[it, d], r, g * 2 + 1 - core)

        for d in order[:2]:
            pair_out(d)
        curve = sym_gram(split(observed), (rounded,))
        curve = curve + unpack(collect(terrain_rows, tbuf.at[it], nr), count)
        curve_cols = cols_out(cbuf.at[it], pack(curve))
        zs = []
        for n, d in enumerate(order):
            own = dot(rounded, block(far[d] * 2 + core), NT)
            if n + 2 < ng:
                pair_out(order[n + 2])
            pairs[d].wait_recv()
            own = own + precv[it, d]
            for i in range(nr):
                zsend[it, d, i] = own[:, i * piece : (i + 1) * piece].astype(BF16)
            for i in range(nr):
                if i or d:
                    to = (r + i) % nr
                    there = far[d] * 2 + core
                    zs.append(send(zsend.at[it, d, to], zrecv.at[it, d, r], to, there))
        zrecv[it, 0, r] = zsend[it, 0, r]
        if it == 0:
            gamma = unpack(collect(gamma_cols, gcol.at[0], nc), count)
        curve = unpack(collect(curve_cols, cbuf.at[it], nc), count)
        if it + 1 < ITERS:
            curve_inv, gamma_inv = inverses([curve, gamma])
        else:
            (curve_inv,) = inverses([curve])
        alpha_t = dot(gamma, curve_inv, NN, HIGH)
        sol[...] += mix(alpha_t, direction[...])
        alpha_both = jnp.concatenate(split(alpha_t), axis=0)
        for copy in zs:
            copy.wait_recv()
        pieces = []
        for i in range(nr):
            total = zrecv[it, 0, i].astype(F32)
            for d in range(1, ng):
                total = total + zrecv[it, d, i].astype(F32)
            pieces.append(total)
        arrived = jnp.concatenate(pieces, axis=1)
        both = dot(jnp.concatenate(split(arrived), axis=0), qt[...])
        image = both[:count] + both[count:] + terrain[...] * direction[...]
        image_hi, image_lo = split(image)
        steps = dot(alpha_both, image_hi)
        residual = res[...] - (steps[:count] + steps[count:] + dot(alpha_both[:count], image_lo))
        res[...] = residual
        if it + 1 < ITERS:
            precon = precondition(residual)

    for copy in sent:
        copy.wait_send()


def part_kernel(both, sol, res):
    sol[...] = both[0]
    res[...] = both[1]


def source_kernel(nr, nc, piece, wanted, out):
    rows = wanted.shape[1]
    high = rows // 128
    chunk = 1024

    def step(i, total):
        w = wanted[:, i * chunk : (i + 1) * chunk]
        owner = w >> bits(piece)
        pos = ((owner & (nc - 1)) * nr + (owner >> bits(nc))) * piece + (w & (piece - 1))
        here = lax.broadcasted_iota(jnp.int32, (high, chunk), 1) + i * chunk
        hit = lax.broadcasted_iota(jnp.int32, (high, chunk), 0) == (pos >> 7)
        upper = jnp.where(hit, (here >> 7).astype(F32), 0.0)
        lower = jnp.where(hit, (here & 127).astype(F32), 0.0)
        lhs = jnp.concatenate([upper, lower], axis=0).astype(BF16)
        lane = lax.broadcasted_iota(jnp.int32, (128, chunk), 0) == (pos & 127)
        return total + dot(lhs, jnp.where(lane, 1.0, 0.0).astype(BF16), NT)

    total = jnp.zeros((2 * high, 128), F32)
    for i in range(rows // chunk):
        total = step(i, total)
    out[...] = (512.0 * total[:high] + 4.0 * total[high:]).astype(jnp.int32)


def source_rows(degree_source, nr, nc, piece):
    rows = degree_source.shape[0]
    vmem = pl.BlockSpec(memory_space=pltpu.VMEM)
    return pl.pallas_call(
        functools.partial(source_kernel, nr, nc, piece),
        out_shape=jax.ShapeDtypeStruct((rows // 128, 128), jnp.int32),
        in_specs=[vmem],
        out_specs=vmem,
    )(degree_source.reshape(1, rows)).reshape(rows)


def place_kernel(steps, chunk, lanes, pos, design, out, stage, placed):
    i = pl.program_id(0)

    @pl.when(i < steps)
    def _():
        for j in range(lanes):
            stage[pl.ds(j, chunk, stride=4), :] = design[:, j * 128 : (j + 1) * 128].astype(F32)
        base = i * chunk

        @pl.loop(0, chunk // 64)
        def _(n):
            for k in range(64):
                row = n * 64 + k
                to = pl.multiple_of(pos[base + row], 4)
                placed[pl.ds(to, 4), :] = stage[pl.ds(pl.multiple_of(row * 4, 4), 4), :]

    @pl.when(i >= steps)
    def _():
        base = pl.multiple_of((i - steps) * (chunk * 4), chunk * 4)
        for j in range(lanes):
            out[:, j * 128 : (j + 1) * 128] = placed[pl.ds(base + j, chunk, stride=4), :].astype(BF16)


def place_rows(design_t, pos):
    rows, obs = design_t.shape
    chunk = 512
    steps = rows // chunk
    return pl.pallas_call(
        functools.partial(place_kernel, steps, chunk, obs // 128),
        grid=(2 * steps,),
        out_shape=jax.ShapeDtypeStruct(design_t.shape, design_t.dtype),
        in_specs=[
            pl.BlockSpec(memory_space=pltpu.SMEM),
            pl.BlockSpec((chunk, obs), lambda i: (jnp.minimum(i, steps - 1), 0)),
        ],
        out_specs=pl.BlockSpec((chunk, obs), lambda i: (jnp.maximum(i - steps, 0), 0)),
        scratch_shapes=[pltpu.VMEM((4 * chunk, 128), F32), pltpu.VMEM((4 * rows, 128), F32)],
        compiler_params=pltpu.CompilerParams(vmem_limit_bytes=48 * 1024 * 1024),
    )(4 * pos, design_t)


def on_device(rhs, precond, design_t, terrain, order_slot, degree_source):
    nr = lax.axis_size("row")
    nc = lax.axis_size("col")
    count, width = rhs.shape
    piece = width // nr
    ng = nc // 2
    obs = design_t.shape[1]
    rows = design_t.shape[0]
    fused = rows <= 8192
    if fused:
        design_g = design_t
        source = source_rows(degree_source, nr, nc, piece)
    else:
        owner = degree_source // piece
        within = degree_source % piece
        design_g = place_rows(design_t, (owner % nc * nr + owner // nc) * piece + within)
        source = degree_source[:128]
    gram = (count * count // 128, 128)
    copies = ITERS * (2 * nr * ng + 3 * nr + 2 * nc + 2 * ng) + nr + nc
    vmem = pl.BlockSpec(memory_space=pltpu.VMEM)
    both = pl.pallas_call(
        functools.partial(kernel, nr, nc, fused),
        out_shape=jax.ShapeDtypeStruct((2,) + rhs.shape, F32),
        in_specs=[
            vmem, pl.BlockSpec(memory_space=pl.ANY), pl.BlockSpec(memory_space=pl.ANY), vmem, vmem,
            pl.BlockSpec(memory_space=pltpu.SMEM),
        ],
        out_specs=vmem,
        scratch_shapes=[
            pltpu.VMEM(design_t.shape, BF16),
            pltpu.SemaphoreType.DMA(()),
            pltpu.VMEM((4 * rows if fused else 8, 128), F32),
            pltpu.VMEM((512, 128), F32),
            pltpu.VMEM((width, width), F32),
            pltpu.SemaphoreType.DMA((width // 128,)),
            pltpu.VMEM((width, width), BF16),
            pltpu.VMEM((width, width), BF16),
            pltpu.VMEM((width, width), BF16),
            pltpu.VMEM((count, width), F32),
            pltpu.VMEM((count, obs), F32),
            pltpu.VMEM((ITERS, nr, count, piece), BF16),
            pltpu.VMEM((ITERS, ng, 2, nr, count, piece), BF16),
            pltpu.VMEM((ITERS, nr, count, obs), BF16),
            pltpu.VMEM((ITERS, ng, count, width), F32),
            pltpu.VMEM((ITERS, ng, count, width), F32),
            pltpu.VMEM((ITERS, ng, nr, count, piece), BF16),
            pltpu.VMEM((ITERS, ng, nr, count, piece), BF16),
            pltpu.VMEM((ITERS, nr) + gram, F32),
            pltpu.VMEM((ITERS, nc) + gram, F32),
            pltpu.VMEM((ITERS, nr) + gram, F32),
            pltpu.VMEM((ITERS, nc) + gram, F32),
            pltpu.SemaphoreType.DMA((copies,)),
            pltpu.SemaphoreType.DMA((copies,)),
        ],
        compiler_params=pltpu.CompilerParams(
            collective_id=0, has_side_effects=True, vmem_limit_bytes=60 * 1024 * 1024
        ),
    )(rhs, precond, design_g, terrain.reshape(1, width), order_slot.reshape(1, width), source)
    return pl.pallas_call(
        part_kernel,
        out_shape=(jax.ShapeDtypeStruct(rhs.shape, F32), jax.ShapeDtypeStruct(rhs.shape, F32)),
        in_specs=[vmem],
        out_specs=(vmem, vmem),
    )(both)


def solution(mesh):
    return jax.shard_map(
        on_device,
        mesh=mesh,
        in_specs=(
            P(None, ("row", "col")),
            P(("row", "col"), None, None),
            P("row", "col"),
            P(("row", "col")),
            P(("row", "col")),
            P("row"),
        ),
        out_specs=(P(None, ("row", "col")), P(None, ("row", "col"))),
        check_vma=False,
    )
```
